128 devices in a mesh: gx: 8 (over z, core), gy: 16 (over y, x).
Axes of the slice: x: 4, y: 4, z: 4, core: 2. Of those that a mesh axis runs over, the one named last changes fastest.
Arguments:
- tiles: bfloat16 [24576, 128, 128], P(('gx', 'gy')), may hold values from -6 to 6
- tile_rows: int32 [24576], P(('gx', 'gy')), may hold values from 0 to 63, as said below
- tile_cols: int32 [24576], P(('gx', 'gy')), may hold values from 0 to 255
- tile_counts: int32 [128], P(('gx', 'gy')), may hold values from 48 to 192
- block_order: int32 [256], replicated, may hold values from 0 to 255, each once
- sketch: bfloat16 [32768, 128], replicated, may hold values from -6 to 6
Outputs:
- cell_factor: bfloat16 [1048576, 128], P(('gx', 'gy'))
- gene_factor: float32 [32768, 128], P(('gx', 'gy'))
The draws below stay inside these ranges and needn't reach their ends.
Inputs may be any that keep to these rules, and one draw needn't show every extreme that they name: On each device the live slots (those below its count) hold distinct coordinate pairs (tile_rows, tile_cols) in increasing lexicographic order; later slots are unused. `block_order`: device d along gx+gy owns the gene blocks in entries d * 2 to (d + 1) * 2 - 1.
All inputs are finite; a program needn't handle non-finite values.
Results may differ from the reference program's by a relative error of at most 0.0019.
Values sent between devices are 32-bit elements; how exact they have to be, the bound alone decides.
A program may use at most 192 MiB of HBM per device.

```python
import math
import jax
import jax.numpy as jnp
from jax import lax

TILE = 128
SKETCH = 128
GENES = 32768
CB_DEV = 64
TILES_DEV = 192
GENE_BLOCKS = 256
CELLS = 1048576
ALL_TILES = 24576
DEVICES = 128


def tile_layout(key):
    base = jax.random.fold_in(key, 11)
    blocks_total = GENES // TILE
    device_ids = jnp.arange(DEVICES, dtype=jnp.int32)
    lowest = TILES_DEV // 3
    linear = lowest + (TILES_DEV - lowest) * device_ids // max(DEVICES - 1, 1)
    jitter = jax.random.randint(jax.random.fold_in(base, 1), (DEVICES,), -(TILES_DEV // 12), TILES_DEV // 12 + 1)
    counts = jnp.clip(linear + jitter, TILES_DEV // 4, TILES_DEV)
    fullest = jax.random.randint(jax.random.fold_in(base, 2), (), 3 * DEVICES // 4, DEVICES)
    counts = jnp.where(device_ids == fullest, TILES_DEV, counts).astype(jnp.int32)
    device_keys = jax.random.split(jax.random.fold_in(base, 3), DEVICES)
    offset = CB_DEV * blocks_total

    def one_device(device_key, live_count):
        codes = jax.random.permutation(device_key, offset)[:TILES_DEV].astype(jnp.int32)
        slots = jnp.arange(TILES_DEV, dtype=jnp.int32)
        shifted = jnp.where(slots < live_count, codes, codes + offset)
        ordered = jnp.sort(shifted)
        return jnp.where(ordered >= offset, ordered - offset, ordered)
    codes = jax.vmap(one_device)(device_keys, counts)
    return (counts, codes.reshape(-1))


def draw_tile_counts(key, part):
    return tile_layout(key)[0]


def draw_tile_rows(key, part):
    return (tile_layout(key)[1] // (GENES // TILE)).astype(jnp.int32)


def draw_tile_cols(key, part):
    return (tile_layout(key)[1] % (GENES // TILE)).astype(jnp.int32)


def shard_levels(own_key, dims, cuts, low, largest):
    loudness = 1.0
    for axis_at, parts in cuts:
        heights = jax.random.uniform(jax.random.fold_in(jax.random.fold_in(own_key, 6), axis_at), (parts,), jnp.float32, low / len(cuts), largest / len(cuts))
        loudness = loudness * jnp.repeat(jnp.exp(heights), dims[axis_at] // parts).reshape((-1,) + (1,) * (len(dims) - 1 - axis_at))
    return loudness


def noise(own_key, dims, deviation, bound, cuts=(), held_as=jnp.bfloat16):
    values = deviation * jax.random.normal(own_key, dims, jnp.float32)
    if cuts:
        values = values * shard_levels(own_key, dims, cuts, -0.22, 0.18)
    return jnp.clip(values, -bound, bound).astype(held_as)


def setup_inputs(seed: int = 0) -> dict:
    streams_of = jax.random.split(jax.random.key(seed), 7)
    return {
        "tiles": noise(streams_of[0], (ALL_TILES, TILE, TILE), 1.0, 6.0, ((0, 128),)),
        "tile_rows": draw_tile_rows(jax.random.fold_in(streams_of[6], 71), 0),
        "tile_cols": draw_tile_cols(jax.random.fold_in(streams_of[6], 71), 0),
        "tile_counts": draw_tile_counts(jax.random.fold_in(streams_of[6], 71), 0),
        "block_order": jax.random.permutation(streams_of[4], GENE_BLOCKS).astype(jnp.int32),
        "sketch": noise(streams_of[5], (GENES, SKETCH), 1.0, 6.0),
    }


def reference(tiles, tile_rows, tile_cols, tile_counts, block_order, sketch):
    blocks_total = GENES // TILE
    tile_sets = tiles.reshape(DEVICES, TILES_DEV, TILE, TILE)
    row_sets = tile_rows.reshape(DEVICES, TILES_DEV)
    col_sets = tile_cols.reshape(DEVICES, TILES_DEV)
    alive = jnp.arange(TILES_DEV, dtype=jnp.int32)[None, :] < tile_counts[:, None]
    sketch_blocks = sketch.reshape(blocks_total, TILE, SKETCH).astype(jnp.float32)

    def cell_part(items):
        tile_block, row_block, col_block, live = items
        product = jnp.einsum('tij,tjs->tis', tile_block.astype(jnp.float32), sketch_blocks[col_block])
        product = jnp.where(live[:, None, None], product, 0.0)
        return jnp.zeros((CB_DEV, TILE, SKETCH), jnp.float32).at[row_block].add(product)
    cell_sum = lax.map(cell_part, (tile_sets, row_sets, col_sets, alive)).reshape(CELLS, SKETCH)
    gram = jnp.dot(cell_sum.T.astype(jnp.float32), cell_sum.astype(jnp.float32), precision=lax.Precision.HIGHEST, preferred_element_type=jnp.float32)
    lower = jnp.linalg.cholesky(gram)
    cell_factor = (math.sqrt(CELLS) * lax.linalg.triangular_solve(lower, cell_sum, left_side=False, lower=True, transpose_a=True)).astype(jnp.bfloat16)
    cell_sets = cell_factor.reshape(DEVICES, CB_DEV, TILE, SKETCH)

    def gene_part(total, items):
        tile_block, row_block, col_block, live, cell_blocks = items
        product = jnp.einsum('tji,tjs->tis', tile_block.astype(jnp.float32), cell_blocks[row_block].astype(jnp.float32))
        product = jnp.where(live[:, None, None], product, 0.0)
        return (total.at[col_block].add(product), None)
    gene_sum, unused = lax.scan(gene_part, jnp.zeros((blocks_total, TILE, SKETCH), jnp.float32), (tile_sets, row_sets, col_sets, alive, cell_sets))
    ordered = gene_sum[block_order].reshape(GENES, SKETCH)
    gram_genes = jnp.dot(ordered.T.astype(jnp.float32), ordered.astype(jnp.float32), precision=lax.Precision.HIGHEST, preferred_element_type=jnp.float32)
    lower_genes = jnp.linalg.cholesky(gram_genes)
    gene_factor = math.sqrt(GENES) * lax.linalg.triangular_solve(lower_genes, ordered, left_side=False, lower=True, transpose_a=True)
    return (cell_factor, gene_factor)
```

```python
import math

import jax
import jax.numpy as jnp
from jax import lax
from jax.experimental import pallas as pl
from jax.experimental.pallas import tpu as pltpu
from jax.sharding import PartitionSpec as P

TILE = 128
SKETCH = 128
GENES = 32768
CB_DEV = 64
BLOCKS = 256
SLOTS = 192
GROUP = 8
CHUNK = 16
F32 = jnp.float32
BF16 = jnp.bfloat16


def local_kernel(counts, rows, cols, order, tiles_hbm, sketch_hbm, split, w_out,
                 tiles, sketch, y_ref, place, tile_sems, sketch_sems):
    live = counts[0]
    w_ref = w_out.reshape(BLOCKS, TILE, SKETCH)
    n_tile = SLOTS // CHUNK
    n_sk = 4
    sk = GENES // n_sk

    def tile_copy(i):
        return pltpu.make_async_copy(
            tiles_hbm.at[pl.ds(i * CHUNK, CHUNK)], tiles.at[pl.ds(i * CHUNK, CHUNK)], tile_sems.at[i])

    def sketch_copy(i):
        return pltpu.make_async_copy(
            sketch_hbm.at[pl.ds(i * sk, sk)], sketch.at[pl.ds(i * sk, sk)], sketch_sems.at[i])

    for i in range(n_sk):
        sketch_copy(i).start()
    for i in range(n_tile):
        tile_copy(i).start()

    def invert(i, _):
        for u in range(8):
            place[order[i * 8 + u]] = i * 8 + u
        return 0
    lax.fori_loop(0, BLOCKS // 8, invert, 0)

    def clear_y(i, _):
        for u in range(4):
            y_ref[i * 4 + u] = jnp.zeros((TILE, SKETCH), F32)
        return 0
    lax.fori_loop(0, CB_DEV // 4, clear_y, 0)

    def clear_w(i, _):
        for u in range(4):
            w_ref[i * 4 + u] = jnp.zeros((TILE, SKETCH), F32)
        return 0
    lax.fori_loop(0, BLOCKS // 4, clear_w, 0)

    for i in range(n_sk):
        sketch_copy(i).wait()

    def cells(i):
        base = i * GROUP
        parts = []
        for u in range(GROUP):
            c = pl.multiple_of(cols[base + u] * TILE, TILE)
            p = jnp.dot(tiles[base + u], sketch[pl.ds(c, TILE), :], preferred_element_type=F32)
            parts.append(jnp.where(base + u < live, p, 0.0))
        for u in range(GROUP):
            r = rows[base + u]
            y_ref[r] = y_ref[r] + parts[u]

    for i in range(n_tile):
        tile_copy(i).wait()

    def cell_body(i, _):
        cells(i)
        return 0
    steps = (live + GROUP - 1) // GROUP
    lax.fori_loop(0, steps, cell_body, 0)

    def cut(i, _):
        for u in range(4):
            v = y_ref[i * 4 + u]
            hi = v.astype(BF16)
            split[i * 4 + u, :, :SKETCH] = hi
            split[i * 4 + u, :, SKETCH:] = (v - hi.astype(F32)).astype(BF16)
        return 0
    lax.fori_loop(0, CB_DEV // 4, cut, 0)

    def gene_body(i, _):
        base = i * GROUP
        parts = []
        for u in range(GROUP):
            r = rows[base + u]
            p = lax.dot_general(tiles[base + u], split[r], (((0,), (0,)), ((), ())),
                                preferred_element_type=F32)
            v = p[:, :SKETCH] + p[:, SKETCH:]
            parts.append(jnp.where(base + u < live, v, 0.0))
        for u in range(GROUP):
            o = place[cols[base + u]]
            w_ref[o] = w_ref[o] + parts[u]
        return 0
    lax.fori_loop(0, steps, gene_body, 0)


def local_pass(tiles, rows, cols, counts, order, sketch):
    smem = pl.BlockSpec(memory_space=pltpu.SMEM)
    anyp = pl.BlockSpec(memory_space=pl.ANY)
    vmem = pl.BlockSpec(memory_space=pltpu.VMEM)
    return pl.pallas_call(
        local_kernel,
        name="local_pass",
        out_shape=(
            pltpu.VMEM((CB_DEV, TILE, 2 * SKETCH), BF16),
            pltpu.VMEM((4, 2, 4, 4, 2 * TILE, SKETCH), F32),
        ),
        in_specs=[smem, smem, smem, smem, anyp, anyp],
        out_specs=(vmem, vmem),
        scratch_shapes=[
            pltpu.VMEM((SLOTS, TILE, TILE), BF16),
            pltpu.VMEM((GENES, SKETCH), BF16),
            pltpu.VMEM((CB_DEV, TILE, SKETCH), F32),
            pltpu.SMEM((BLOCKS,), jnp.int32),
            pltpu.SemaphoreType.DMA((SLOTS // CHUNK,)),
            pltpu.SemaphoreType.DMA((4,)),
        ],
        compiler_params=pltpu.CompilerParams(vmem_limit_bytes=24 << 20),
    )(counts, rows, cols, order, tiles, sketch)


PARTS = ((0, 88), (88, 88), (176, 80))
ORDERS = ((2, 1, 0), (1, 0, 2), (0, 2, 1))
MESH = pl.DeviceIdType.MESH
HIGH = lax.Precision.HIGHEST


def cut_two(v):
    hi = v.astype(BF16)
    return hi, (v - hi.astype(F32)).astype(BF16)


def inverse_factor(gram, work, out):
    work[:, :SKETCH] = gram[...]
    ri = lax.broadcasted_iota(jnp.int32, (SKETCH, SKETCH), 0)
    ci = lax.broadcasted_iota(jnp.int32, (SKETCH, SKETCH), 1)
    work[:, SKETCH:] = jnp.where(ri == ci, 1.0, 0.0)
    lane = lax.broadcasted_iota(jnp.int32, (1, SKETCH), 1)
    down = lax.broadcasted_iota(jnp.int32, (SKETCH, 1), 0)

    def body(j, carry):
        row = work[pl.ds(j, 1), :]
        left = work[:, :SKETCH]
        pivot = jnp.sum(jnp.where(lane == j, row[:, :SKETCH], 0.0), axis=1, keepdims=True)
        col = jnp.sum(jnp.where(ci == j, left, 0.0), axis=1, keepdims=True)
        mult = jnp.where(down > j, col, 0.0)
        scaled = row / pivot
        work[:, :SKETCH] = left - mult * scaled[:, :SKETCH]
        work[:, SKETCH:] = work[:, SKETCH:] - mult * scaled[:, SKETCH:]
        return carry

    lax.fori_loop(0, SKETCH, body, 0)
    diag = jnp.sum(jnp.where(ri == ci, work[:, :SKETCH], 0.0), axis=1, keepdims=True)
    out[...] = work[:, SKETCH:] / jnp.sqrt(diag)


def exchange_kernel(split, w, cell_out, gene_out,
                    acc, box1, box2, box3, cell, gram, total, work, inv1, inv2, zed,
                    cur, first, slots,
                    in_send, in_recv, ring_send, ring_recv, sum_send, sum_recv, out_sem):
    gx = lax.axis_index("gx")
    gy = lax.axis_index("gy")
    z, core = gx // 2, gx % 2
    y, x = gy // 4, gy % 4
    me = (z, y, x)

    def device(pos, c):
        return (pos[0] * 2 + c, pos[1] * 4 + pos[2])

    def moved(axis, k):
        pos = list(me)
        pos[axis] = (pos[axis] + k + 4) % 4
        return pos

    partner = device(me, 1 - core)
    barrier = pltpu.get_barrier_semaphore()
    peers = [partner] + [device(moved(a, k), core) for a in range(3) for k in (1, 2, 3)]
    for peer in peers:
        pl.semaphore_signal(barrier, inc=1, device_id=peer, device_id_type=MESH)
    pl.semaphore_wait(barrier, len(peers))

    def remote(src, dst, send, recv, peer):
        return pltpu.make_async_remote_copy(
            src_ref=src, dst_ref=dst, send_sem=send, recv_sem=recv,
            device_id=peer, device_id_type=MESH)

    def at(fixed, part, halves=None, rows=None):
        idx = [fixed.get(d, slice(None)) for d in range(3)]
        free = [d for d in range(3) if d not in fixed]
        if halves is not None and free:
            idx[free[0]] = pl.ds(2 * halves, 2)
        r0, nr = PARTS[part]
        if rows is not None:
            r0, nr = r0 + rows[0], rows[1]
        idx.append(pl.ds(r0, nr))
        return tuple(idx)

    def add(dst, src, lead):
        if len(lead) == 2:
            n = lead[1]

            def body(i, carry):
                a, b = i // n, i % n
                dst[a, b] = dst[a, b] + src[a, b]
                return carry
            lax.fori_loop(0, lead[0] * n, body, 0)
        elif len(lead) == 1:
            def body1(i, carry):
                dst[i] = dst[i] + src[i]
                return carry
            lax.fori_loop(0, lead[0], body1, 0)
        else:
            dst[...] = dst[...] + src[...]

    def with_core(idx, c):
        return (idx[0], c) + tuple(idx[1:])

    steps = (2, 1, 3, 0)
    pieces = {}
    for n, k in enumerate(steps):
        for p in range(3):
            a = ORDERS[p][0]
            idx = at({a: (me[a] + k) % 4}, p)
            copy = remote(w.at[with_core(idx, 1 - core)], acc.at[idx],
                          in_send.at[n * 3 + p], in_recv.at[n * 3 + p], partner)
            copy.start()
            pieces[k, p] = copy, idx

    def gram_body(i, g):
        v = split[pl.ds(i * 8, 8)].reshape(8 * TILE, 2 * SKETCH)
        return g + lax.dot_general(v, v, (((0,), (0,)), ((), ())), preferred_element_type=F32)
    g = lax.fori_loop(0, CB_DEV // 8, gram_body, jnp.zeros((2 * SKETCH, 2 * SKETCH), F32))
    gram[...] = (g[:SKETCH, :SKETCH] + g[SKETCH:, SKETCH:]) + (g[:SKETCH, SKETCH:] + g[SKETCH:, :SKETCH])

    half = SKETCH // 2

    def sum_start(w_):
        copy = remote(gram.at[pl.ds((1 - core) * half, half)], first.at[w_],
                      sum_send.at[w_, 9], sum_recv.at[w_, 9], partner)
        copy.start()
        return copy

    def sum_send_axis(w_, a, value):
        cur[w_, a] = value
        slots[w_, a, me[a]] = value
        copies = []
        for k in (1, 2, 3):
            copy = remote(cur.at[w_, a], slots.at[w_, a, me[a]],
                          sum_send.at[w_, a * 3 + k - 1], sum_recv.at[w_, a * 3 + k - 1],
                          device(moved(a, k), core))
            copy.start()
            copies.append(copy)
        return copies

    def sum_axis(w_, a, copies):
        for copy in copies:
            copy.wait()
        return (slots[w_, a, 0] + slots[w_, a, 1]) + (slots[w_, a, 2] + slots[w_, a, 3])

    def sum_first(w_, copy):
        copy.wait()
        return gram[pl.ds(core * half, half), :] + first[w_]

    def sum_last(w_, value):
        mine = pl.ds(core * half, half)
        cur[w_, 3] = value
        total[w_, mine, :] = value
        copy = remote(cur.at[w_, 3], total.at[w_, mine], sum_send.at[w_, 10], sum_recv.at[w_, 10], partner)
        copy.start()
        return copy

    g0 = sum_start(0)

    HALF_ROWS = ((0, 48), (48, None))
    boxes = (box1, box2, box3)
    fixed = [dict() for _ in range(3)]

    def span(phase, p, h):
        nr = PARTS[p][1]
        if phase < 2:
            return None, nr
        return ((0, 48), 48) if h == 0 else ((48, nr - 48), nr - 48)

    def view(phase, p, coord, h):
        f = dict(fixed[p])
        f[ORDERS[p][phase]] = coord
        rows, nr = span(phase, p, h)
        return acc.at[at(f, p, h, rows)]

    def box(phase, p, m, h):
        nr = span(phase, p, h)[1]
        b = boxes[phase]
        if phase == 0:
            return b.at[p, m, :, :, pl.ds(0, nr)]
        if phase == 1:
            return b.at[p, m, :, pl.ds(0, nr)]
        return b.at[p, m, pl.ds(0, nr)]

    leads = ((2, 4), (2,), ())

    def send(phase, p, m):
        a = ORDERS[p][phase]
        sign = 1 if m % 2 == 0 else -1
        coord = (me[a] + (2 if m < 2 else sign) + 4) % 4
        h = (0, 1, 1, 0, 0, 1)[m]
        copy = remote(view(phase, p, coord, h), box(phase, p, m, h),
                      ring_send.at[phase, p * 6 + m], ring_recv.at[phase, p * 6 + m],
                      device(moved(a, sign), core))
        copy.start()
        return copy

    def pass_on(phase, p, m, copy):
        a = ORDERS[p][phase]
        sign = 1 if m % 2 == 0 else -1
        h = m % 2
        copy.wait_recv()
        add(view(phase, p, (me[a] + sign + 4) % 4, h), box(phase, p, m, h), leads[phase])

    def land(phase, p, m, copy):
        a = ORDERS[p][phase]
        h = (0, 1, 1, 0, 0, 1)[m]
        copy.wait_recv()
        add(view(phase, p, me[a], h), box(phase, p, m, h), leads[phase])

    def merge(k, p):
        copy, idx = pieces[k, p]
        copy.wait()
        add(acc.at[idx], w.at[with_core(idx, core)], (4, 4))

    ring = {}
    for p in range(3):
        merge(2, p)
        ring[0, p, 0] = send(0, p, 0)
        ring[0, p, 1] = send(0, p, 1)
    gx_ = sum_send_axis(0, 2, sum_first(0, g0))
    for p in range(3):
        merge(1, p)
        ring[0, p, 2] = send(0, p, 2)
        merge(3, p)
        ring[0, p, 3] = send(0, p, 3)
    gy_ = sum_send_axis(0, 1, sum_axis(0, 2, gx_))
    for p in range(3):
        for m in (0, 1):
            pass_on(0, p, m, ring[0, p, m])
            ring[0, p, 4 + m] = send(0, p, 4 + m)
    gz_ = sum_send_axis(0, 0, sum_axis(0, 1, gy_))
    for p in range(3):
        merge(0, p)
    gl_ = sum_last(0, sum_axis(0, 0, gz_))
    gl_.wait()

    inverse_factor(total.at[0], work, inv1)
    lh, ll = cut_two(inv1[...] * math.sqrt(CB_DEV * TILE * 128))
    weights = jnp.concatenate(
        [jnp.concatenate([lh, lh], axis=1), jnp.concatenate([ll, jnp.zeros_like(ll)], axis=1)], axis=0)

    def cell_body(i, carry):
        v = split[pl.ds(i * 4, 4)].reshape(4 * TILE, 2 * SKETCH)
        o = lax.dot_general(v, weights, (((1,), (1,)), ((), ())), preferred_element_type=F32)
        cell[pl.ds(pl.multiple_of(i * 4 * TILE, 4 * TILE), 4 * TILE), :] = (
            o[:, :SKETCH] + o[:, SKETCH:]).astype(BF16)
        return carry
    lax.fori_loop(0, CB_DEV // 4, cell_body, 0)
    out_copy = pltpu.make_async_copy(cell, cell_out, out_sem.at[0])
    out_copy.start()

    for phase in range(3):
        if phase:
            for p in range(3):
                for m in range(4):
                    ring[phase, p, m] = send(phase, p, m)
            for p in range(3):
                for m in (0, 1):
                    pass_on(phase, p, m, ring[phase, p, m])
                    ring[phase, p, 4 + m] = send(phase, p, 4 + m)
        for m in (2, 3, 4, 5):
            for p in range(3):
                land(phase, p, m, ring[phase, p, m])
        for p in range(3):
            for m in range(6):
                ring[phase, p, m].wait_send()
            fixed[p][ORDERS[p][phase]] = me[ORDERS[p][phase]]

    own = acc[z, y, x]
    zv = lax.dot_general(own, inv1[...], (((1,), (1,)), ((), ())), precision=HIGH, preferred_element_type=F32)
    zed[...] = zv
    gram[...] = lax.dot_general(zv, zv, (((0,), (0,)), ((), ())), precision=HIGH, preferred_element_type=F32)
    value = sum_first(1, sum_start(1))
    for a in (2, 1, 0):
        value = sum_axis(1, a, sum_send_axis(1, a, value))
    sum_last(1, value).wait()
    inverse_factor(total.at[1], work, inv2)
    gene_out[...] = math.sqrt(GENES) * lax.dot_general(
        zed[...], inv2[...], (((1,), (1,)), ((), ())), precision=HIGH, preferred_element_type=F32)
    out_copy.wait()


def exchange(split, w):
    vmem = pl.BlockSpec(memory_space=pltpu.VMEM)
    sq = (SKETCH, SKETCH)
    return pl.pallas_call(
        exchange_kernel,
        name="exchange",
        out_shape=(
            jax.ShapeDtypeStruct((CB_DEV * TILE, SKETCH), BF16),
            jax.ShapeDtypeStruct((2 * TILE, SKETCH), F32),
        ),
        in_specs=[vmem, vmem],
        out_specs=(pl.BlockSpec(memory_space=pl.ANY), vmem),
        scratch_shapes=[
            pltpu.VMEM((4, 4, 4, 2 * TILE, SKETCH), F32),
            pltpu.VMEM((3, 6, 2, 4, 88, SKETCH), F32),
            pltpu.VMEM((3, 6, 2, 88, SKETCH), F32),
            pltpu.VMEM((3, 6, 48, SKETCH), F32),
            pltpu.VMEM((CB_DEV * TILE, SKETCH), BF16),
            pltpu.VMEM(sq, F32),
            pltpu.VMEM((2,) + sq, F32),
            pltpu.VMEM((SKETCH, 2 * SKETCH), F32),
            pltpu.VMEM(sq, F32),
            pltpu.VMEM(sq, F32),
            pltpu.VMEM((2 * TILE, SKETCH), F32),
            pltpu.VMEM((2, 4, SKETCH // 2, SKETCH), F32),
            pltpu.VMEM((2, SKETCH // 2, SKETCH), F32),
            pltpu.VMEM((2, 3, 4, SKETCH // 2, SKETCH), F32),
            pltpu.SemaphoreType.DMA((12,)),
            pltpu.SemaphoreType.DMA((12,)),
            pltpu.SemaphoreType.DMA((3, 18)),
            pltpu.SemaphoreType.DMA((3, 18)),
            pltpu.SemaphoreType.DMA((2, 11)),
            pltpu.SemaphoreType.DMA((2, 11)),
            pltpu.SemaphoreType.DMA((1,)),
        ],
        compiler_params=pltpu.CompilerParams(
            collective_id=0, has_side_effects=True, vmem_limit_bytes=26 << 20),
    )(pltpu.with_memory_space_constraint(split, pltpu.VMEM), pltpu.with_memory_space_constraint(w, pltpu.VMEM))


def on_device(tiles, tile_rows, tile_cols, tile_counts, block_order, sketch):
    split, w = local_pass(tiles, tile_rows, tile_cols, tile_counts, block_order, sketch)
    return exchange(split, w)


def solution(mesh):
    placed = (
        P(("gx", "gy"), None, None),
        P(("gx", "gy")),
        P(("gx", "gy")),
        P(("gx", "gy")),
        P(),
        P(),
    )
    return jax.shard_map(
        on_device,
        mesh=mesh,
        in_specs=placed,
        out_specs=(P(("gx", "gy"), None), P(("gx", "gy"), None)),
        check_vma=False,
    )
```

```python
import math

import jax
import jax.numpy as jnp
from jax import lax
from jax.experimental import pallas as pl
from jax.experimental.pallas import tpu as pltpu
from jax.sharding import PartitionSpec as P

TILE = 128
SKETCH = 128
GENES = 32768
CB_DEV = 64
BLOCKS = 256
SLOTS = 192
GROUP = 8
CHUNK = 16
F32 = jnp.float32
BF16 = jnp.bfloat16


def local_kernel(counts, rows_hbm, cols_hbm, order_hbm, tiles_hbm, sketch_hbm, split, w_out,
                 tiles, sketch, y_ref, place, rows, cols, order,
                 tile_sems, sketch_sems, index_sems):
    lists = ((rows_hbm, rows), (cols_hbm, cols), (order_hbm, order))
    index_copies = [pltpu.make_async_copy(a, b, index_sems.at[i]) for i, (a, b) in enumerate(lists)]
    for copy in index_copies:
        copy.start()
    w_ref = w_out.reshape(BLOCKS, TILE, SKETCH)
    n_tile = SLOTS // CHUNK
    n_sk = 4
    sk = GENES // n_sk

    def tile_copy(i):
        return pltpu.make_async_copy(
            tiles_hbm.at[pl.ds(i * CHUNK, CHUNK)], tiles.at[pl.ds(i * CHUNK, CHUNK)], tile_sems.at[i])

    def sketch_copy(i):
        return pltpu.make_async_copy(
            sketch_hbm.at[pl.ds(i * sk, sk)], sketch.at[pl.ds(i * sk, sk)], sketch_sems.at[i])

    for i in range(n_sk):
        sketch_copy(i).start()
    for i in range(n_tile):
        tile_copy(i).start()

    for copy in index_copies:
        copy.wait()
    live = counts[0]

    def invert(i, _):
        for u in range(8):
            place[order[i * 8 + u]] = i * 8 + u
        return 0
    lax.fori_loop(0, BLOCKS // 8, invert, 0)

    def clear_y(i, _):
        for u in range(4):
            y_ref[i * 4 + u] = jnp.zeros((TILE, SKETCH), F32)
        return 0
    lax.fori_loop(0, CB_DEV // 4, clear_y, 0)

    def clear_w(i, _):
        for u in range(4):
            w_ref[i * 4 + u] = jnp.zeros((TILE, SKETCH), F32)
        return 0
    lax.fori_loop(0, BLOCKS // 4, clear_w, 0)

    for i in range(n_sk):
        sketch_copy(i).wait()

    def cells(i):
        base = i * GROUP
        parts = []
        for u in range(GROUP):
            c = pl.multiple_of(cols[base + u] * TILE, TILE)
            p = jnp.dot(tiles[base + u], sketch[pl.ds(c, TILE), :], preferred_element_type=F32)
            parts.append(jnp.where(base + u < live, p, 0.0))
        for u in range(GROUP):
            r = rows[base + u]
            y_ref[r] = y_ref[r] + parts[u]

    def cell_body(i, _):
        @pl.when(i % (CHUNK // GROUP) == 0)
        def _():
            tile_copy(i // (CHUNK // GROUP)).wait()
        cells(i)
        return 0
    steps = (live + GROUP - 1) // GROUP
    lax.fori_loop(0, steps, cell_body, 0)

    def late(i, _):
        tile_copy(i).wait()
        return 0
    lax.fori_loop((live + CHUNK - 1) // CHUNK, n_tile, late, 0)

    def cut(i, _):
        for u in range(4):
            v = y_ref[i * 4 + u]
            hi = v.astype(BF16)
            split[i * 4 + u, :, :SKETCH] = hi
            split[i * 4 + u, :, SKETCH:] = (v - hi.astype(F32)).astype(BF16)
        return 0
    lax.fori_loop(0, CB_DEV // 4, cut, 0)

    def gene_body(i, _):
        base = i * GROUP
        parts = []
        for u in range(GROUP):
            r = rows[base + u]
            p = lax.dot_general(tiles[base + u], split[r], (((0,), (0,)), ((), ())),
                                preferred_element_type=F32)
            v = p[:, :SKETCH] + p[:, SKETCH:]
            parts.append(jnp.where(base + u < live, v, 0.0))
        for u in range(GROUP):
            o = place[cols[base + u]]
            w_ref[o] = w_ref[o] + parts[u]
        return 0
    lax.fori_loop(0, steps, gene_body, 0)


def local_pass(tiles, rows, cols, counts, order, sketch):
    hbm = [pltpu.with_memory_space_constraint(v, pltpu.HBM) for v in (rows, cols, order, tiles, sketch)]
    anyp = pl.BlockSpec(memory_space=pl.ANY)
    vmem = pl.BlockSpec(memory_space=pltpu.VMEM)
    return pl.pallas_call(
        local_kernel,
        name="local_pass",
        out_shape=(
            pltpu.VMEM((CB_DEV, TILE, 2 * SKETCH), BF16),
            pltpu.VMEM((4, 2, 4, 4, 2 * TILE, SKETCH), F32),
        ),
        in_specs=[pl.BlockSpec(memory_space=pltpu.SMEM)] + [anyp] * 5,
        out_specs=(vmem, vmem),
        scratch_shapes=[
            pltpu.VMEM((SLOTS, TILE, TILE), BF16),
            pltpu.VMEM((GENES, SKETCH), BF16),
            pltpu.VMEM((CB_DEV, TILE, SKETCH), F32),
            pltpu.SMEM((BLOCKS,), jnp.int32),
            pltpu.SMEM((SLOTS,), jnp.int32),
            pltpu.SMEM((SLOTS,), jnp.int32),
            pltpu.SMEM((BLOCKS,), jnp.int32),
            pltpu.SemaphoreType.DMA((SLOTS // CHUNK,)),
            pltpu.SemaphoreType.DMA((4,)),
            pltpu.SemaphoreType.DMA((4,)),
        ],
        compiler_params=pltpu.CompilerParams(vmem_limit_bytes=26 << 20),
    )(counts, *hbm)


PARTS = ((0, 88), (88, 88), (176, 80))
ORDERS = ((2, 1, 0), (1, 0, 2), (0, 2, 1))
ROUNDS = (2, 1, 3, 0)
TURN = (0, 1, 1, 0, 0, 1)
MESH = pl.DeviceIdType.MESH
HIGH = lax.Precision.HIGHEST


def cut_two(v):
    hi = v.astype(BF16)
    return hi, (v - hi.astype(F32)).astype(BF16)


WINDOW = 4


def factor_start(gram, work):
    work[:, :SKETCH] = gram[...]
    ri = lax.broadcasted_iota(jnp.int32, (SKETCH, SKETCH), 0)
    ci = lax.broadcasted_iota(jnp.int32, (SKETCH, SKETCH), 1)
    work[:, SKETCH:] = jnp.where(ri == ci, 1.0, 0.0)


def factor_steps(work, out, first, last):
    rows = 32
    down = lax.broadcasted_iota(jnp.int32, (rows, 1), 0)

    def lane(v, n):
        return jnp.broadcast_to(v[:, n:n + 1], (v.shape[0], SKETCH))

    def group(j, l0):
        tile = pl.ds(pl.multiple_of(j, 8), 8)
        lt = work[tile, :SKETCH]
        rt = work[tile, SKETCH:]
        left = [jnp.broadcast_to(lt[l0 + t:l0 + t + 1], (8, SKETCH)) for t in range(WINDOW)]
        right = [jnp.broadcast_to(rt[l0 + t:l0 + t + 1], (8, SKETCH)) for t in range(WINDOW)]
        e = {(s, t): lane(left[s], l0 + t) for s in range(WINDOW) for t in range(s, WINDOW)}
        w = {}
        inv = []
        for s in range(WINDOW):
            inv.append(1.0 / e[s, s])
            for t in range(s + 1, WINDOW):
                w[s, t] = e[s, t] * inv[s]
            for t in range(s + 1, WINDOW):
                for u in range(t, WINDOW):
                    e[t, u] = e[t, u] - w[s, t] * e[s, u]
                left[t] = left[t] - w[s, t] * left[s]
                right[t] = right[t] - w[s, t] * right[s]
        done = [right[t] * (1.0 / jnp.sqrt(e[t, t])) for t in range(WINDOW)]
        ql = [(left[t] * inv[t])[:1] for t in range(WINDOW)]
        qr = [(right[t] * inv[t])[:1] for t in range(WINDOW)]
        ww = {k: v[:1] for k, v in w.items()}
        for i in range(SKETCH // rows):
            here = pl.ds(i * rows, rows)
            a = work[here, :SKETCH]
            b = work[here, SKETCH:]
            below = down + i * rows > j + l0 + WINDOW - 1
            c = [jnp.where(below, lane(a, l0 + t), 0.0) for t in range(WINDOW)]
            for t in range(1, WINDOW):
                for s in range(t):
                    c[t] = c[t] - c[s] * ww[s, t]
            for t in range(WINDOW):
                a = a - c[t] * ql[t]
                b = b - c[t] * qr[t]
            if l0 + WINDOW == 8:
                a = pltpu.roll(a, SKETCH - 8, 1)
            work[here, :SKETCH] = a
            work[here, SKETCH:] = b
        return done

    sub = lax.broadcasted_iota(jnp.int32, (8, 1), 0)

    def body(i, carry):
        done = []
        for l0 in range(0, 8, WINDOW):
            done += group(i * 8, l0)
        tile = done[0]
        for t in range(1, 8):
            tile = jnp.where(sub == t, done[t], tile)
        out[pl.ds(pl.multiple_of(i * 8, 8), 8), :] = tile
        return carry

    lax.fori_loop(first, last, body, 0)


def exchange_kernel(split, w, cell_out, gene_out,
                    acc, box1, box2, box3, cell, gram, total, work, inv1, inv2, zed,
                    cur, first, slots,
                    in_send, in_recv, ring_send, ring_recv, sum_send, sum_recv, out_sem):
    gx = lax.axis_index("gx")
    gy = lax.axis_index("gy")
    z, core = gx // 2, gx % 2
    y, x = gy // 4, gy % 4
    me = (z, y, x)

    def device(pos, c):
        return (pos[0] * 2 + c, pos[1] * 4 + pos[2])

    def around(axis, k):
        return (me[axis] + k + 4) % 4

    def moved(axis, k):
        pos = list(me)
        pos[axis] = around(axis, k)
        return pos

    near = [(dx, dc) for dx in range(4) for dc in range(2) if dx or dc]

    def near_device(dx, dc):
        return device(moved(2, dx), 1 - core if dc else core)

    partner = near_device(0, 1)
    barrier = pltpu.get_barrier_semaphore()
    peers = [near_device(dx, dc) for dx, dc in near]
    peers += [device(moved(a, k), core) for a in (0, 1) for k in (1, 2, 3)]
    for peer in peers:
        pl.semaphore_signal(barrier, inc=1, device_id=peer, device_id_type=MESH)
    pl.semaphore_wait(barrier, len(peers))

    sends = []

    def remote(src, dst, send, recv, peer):
        copy = pltpu.make_async_remote_copy(
            src_ref=src, dst_ref=dst, send_sem=send, recv_sem=recv,
            device_id=peer, device_id_type=MESH)
        copy.start()
        sends.append(copy)
        return copy

    def add(dst, src, lead):
        if lead:
            def body(i, carry):
                dst[i] = dst[i] + src[i]
                return carry
            lax.fori_loop(0, lead, body, 0)
        else:
            dst[...] = dst[...] + src[...]

    def place(p, ca, cb, cc, rows=None):
        idx = [None] * 3
        for d, v in zip(ORDERS[p], (ca, cb, cc)):
            idx[d] = v
        r0, nr = PARTS[p]
        if rows is not None:
            r0, nr = r0 + rows[0], rows[1]
        return tuple(idx) + (pl.ds(r0, nr),)

    def with_core(idx, c):
        return (idx[0], c) + tuple(idx[1:])

    pieces = {}

    def piece(k, q, p):
        n = (k * 4 + q) * 3 + p
        a, b = ORDERS[p][:2]
        idx = place(p, around(a, k), around(b, q), slice(None))
        pieces[k, q, p] = idx, remote(w.at[with_core(idx, 1 - core)], acc.at[idx],
                                      in_send.at[n], in_recv.at[n], partner)

    def merge(k, q, p):
        idx, copy = pieces[k, q, p]
        copy.wait_recv()
        add(acc.at[idx], w.at[with_core(idx, core)], 4)

    share = SKETCH // 8
    mine = pl.ds((x * 2 + core) * share, share)

    def sum_start(s):
        first[s, x * 2 + core] = gram[s, mine, :]
        out = []
        for dx, dc in near:
            n = dx * 2 + dc
            to = around(2, dx) * 2 + ((1 - core) if dc else core)
            out.append(remote(gram.at[s, pl.ds(to * share, share)], first.at[s, x * 2 + core],
                              sum_send.at[s, n], sum_recv.at[s, n], near_device(dx, dc)))
        return out

    def landed(copies):
        for copy in copies:
            copy.wait_recv()

    def sum_along(s, a, value):
        cur[s, a] = value
        slots[s, a, me[a]] = value
        out = []
        for k in (1, 2, 3):
            n = 7 + a * 3 + k
            out.append(remote(cur.at[s, a], slots.at[s, a, me[a]], sum_send.at[s, n], sum_recv.at[s, n],
                              device(moved(a, k), core)))
        return out

    def sum_first(s, copies):
        landed(copies)
        v = [first[s, n] for n in range(8)]
        return ((v[0] + v[1]) + (v[2] + v[3])) + ((v[4] + v[5]) + (v[6] + v[7]))

    def sum_next(s, a, copies):
        landed(copies)
        return (slots[s, a, 0] + slots[s, a, 1]) + (slots[s, a, 2] + slots[s, a, 3])

    def sum_spread(s, value):
        cur[s, 2] = value
        total[s, mine, :] = value
        out = []
        for dx, dc in near:
            n = 13 + dx * 2 + dc
            out.append(remote(cur.at[s, 2], total.at[s, mine], sum_send.at[s, n], sum_recv.at[s, n],
                              near_device(dx, dc)))
        return out

    ring = {}

    def half(h):
        return pl.ds(2 * h, 2)

    def view(phase, p, q, coord, h):
        a, b, c = ORDERS[p]
        if phase == 0:
            return acc.at[place(p, coord, around(b, q), half(h))]
        if phase == 1:
            return acc.at[place(p, me[a], coord, half(h))]
        return acc.at[place(p, me[a], me[b], coord, tail(p, h))]

    def tail(p, h):
        return (0, 48) if h == 0 else (48, PARTS[p][1] - 48)

    def box(phase, p, q, m, h):
        nr = PARTS[p][1]
        if phase == 0:
            return box1.at[p, q, m, :, pl.ds(0, nr)]
        if phase == 1:
            return box2.at[p, m, :, pl.ds(0, nr)]
        return box3.at[p, m, pl.ds(0, tail(p, h)[1])]

    def send(phase, p, q, m):
        axis = ORDERS[p][phase]
        sign = 1 if m % 2 == 0 else -1
        h = TURN[m]
        n = (p * 4 + q) * 6 + m if phase == 0 else 72 + (phase - 1) * 18 + p * 6 + m
        ring[phase, p, q, m] = remote(
            view(phase, p, q, around(axis, 2 if m < 2 else sign), h), box(phase, p, q, m, h),
            ring_send.at[n], ring_recv.at[n], device(moved(axis, sign), core))

    def relay(phase, p, q, m):
        axis = ORDERS[p][phase]
        sign = 1 if m == 0 else -1
        ring[phase, p, q, m].wait_recv()
        add(view(phase, p, q, around(axis, sign), m), box(phase, p, q, m, m), 0 if phase == 2 else 2)
        send(phase, p, q, 4 + m)

    def land(phase, p, q, m):
        ring[phase, p, q, m].wait_recv()
        add(view(phase, p, q, me[ORDERS[p][phase]], TURN[m]), box(phase, p, q, m, TURN[m]),
            0 if phase == 2 else 2)

    def open_round(q):
        for p in range(3):
            merge(2, q, p)
            send(0, p, q, 0)
            send(0, p, q, 1)
        for p in range(3):
            merge(1, q, p)
            send(0, p, q, 2)
            merge(3, q, p)
            send(0, p, q, 3)

    def relay_round(q):
        for p in range(3):
            relay(0, p, q, 0)
            relay(0, p, q, 1)

    def close_round(q):
        for p in range(3):
            merge(0, q, p)
        for m in (2, 3, 4, 5):
            for p in range(3):
                land(0, p, q, m)
        for p in range(3):
            if q == 2:
                send(1, p, 0, 0)
                send(1, p, 0, 1)
            elif q == 1:
                send(1, p, 0, 2)
            elif q == 3:
                send(1, p, 0, 3)
        if q in (1, 3):
            for p in range(3):
                relay(1, p, 0, 0 if q == 1 else 1)

    for k in ROUNDS:
        for p in range(3):
            piece(k, 2, p)

    def gram_body(i, g):
        v = split[pl.ds(i * 8, 8)].reshape(8 * TILE, 2 * SKETCH)
        return g + lax.dot_general(v, v, (((0,), (0,)), ((), ())), preferred_element_type=F32)
    g = lax.fori_loop(0, CB_DEV // 8, gram_body, jnp.zeros((2 * SKETCH, 2 * SKETCH), F32))
    gram[0] = (g[:SKETCH, :SKETCH] + g[SKETCH:, SKETCH:]) + (g[:SKETCH, SKETCH:] + g[SKETCH:, :SKETCH])
    copies = sum_start(0)
    for q in ROUNDS[1:]:
        for k in ROUNDS:
            for p in range(3):
                piece(k, q, p)

    open_round(2)
    copies = sum_along(0, 1, sum_first(0, copies))
    open_round(1)
    relay_round(2)
    copies = sum_along(0, 0, sum_next(0, 1, copies))
    open_round(3)
    relay_round(1)
    close_round(2)
    copies = sum_spread(0, sum_next(0, 0, copies))
    open_round(0)
    relay_round(3)
    close_round(1)
    landed(copies)
    factor_start(total.at[0], work)
    factor_steps(work, inv1, 0, 5)
    relay_round(0)
    factor_steps(work, inv1, 5, 10)
    close_round(3)
    factor_steps(work, inv1, 10, 16)
    close_round(0)
    for m in (2, 3, 4, 5):
        for p in range(3):
            land(1, p, 0, m)
    for m in range(4):
        for p in range(3):
            send(2, p, 0, m)
    lh, ll = cut_two(inv1[...] * math.sqrt(CB_DEV * TILE * 128))
    weights = jnp.concatenate(
        [jnp.concatenate([lh, lh], axis=1), jnp.concatenate([ll, jnp.zeros_like(ll)], axis=1)], axis=0)
    for p in range(3):
        relay(2, p, 0, 0)
        relay(2, p, 0, 1)
    for m in (2, 3, 4, 5):
        for p in range(3):
            land(2, p, 0, m)

    zv = lax.dot_general(acc[z, y, x], inv1[...], (((1,), (1,)), ((), ())),
                         precision=HIGH, preferred_element_type=F32)
    zed[...] = zv
    gram[1] = lax.dot_general(zv, zv, (((0,), (0,)), ((), ())), precision=HIGH, preferred_element_type=F32)

    out_copies = []

    def cells(n):
        def body(i, carry):
            v = split[pl.ds(i * 4, 4)].reshape(4 * TILE, 2 * SKETCH)
            o = lax.dot_general(v, weights, (((1,), (1,)), ((), ())), preferred_element_type=F32)
            cell[pl.ds(pl.multiple_of(i * 4 * TILE, 4 * TILE), 4 * TILE), :] = (
                o[:, :SKETCH] + o[:, SKETCH:]).astype(BF16)
            return carry
        lax.fori_loop(n * 4, n * 4 + 4, body, 0)
        rows = pl.ds(n * 16 * TILE, 16 * TILE)
        copy = pltpu.make_async_copy(cell.at[rows], cell_out.at[rows], out_sem.at[n])
        copy.start()
        out_copies.append(copy)

    copies = sum_start(1)
    cells(0)
    copies = sum_along(1, 1, sum_first(1, copies))
    cells(1)
    copies = sum_along(1, 0, sum_next(1, 1, copies))
    cells(2)
    copies = sum_spread(1, sum_next(1, 0, copies))
    cells(3)
    landed(copies)
    factor_start(total.at[1], work)
    factor_steps(work, inv2, 0, 16)
    gene_out[...] = math.sqrt(GENES) * lax.dot_general(
        zed[...], inv2[...], (((1,), (1,)), ((), ())), precision=HIGH, preferred_element_type=F32)
    for copy in sends:
        copy.wait_send()
    for copy in out_copies:
        copy.wait()


def exchange(split, w):
    vmem = pl.BlockSpec(memory_space=pltpu.VMEM)
    sq = (SKETCH, SKETCH)
    part = (SKETCH // 8, SKETCH)
    return pl.pallas_call(
        exchange_kernel,
        name="exchange",
        out_shape=(
            jax.ShapeDtypeStruct((CB_DEV * TILE, SKETCH), BF16),
            jax.ShapeDtypeStruct((2 * TILE, SKETCH), F32),
        ),
        in_specs=[vmem, vmem],
        out_specs=(pl.BlockSpec(memory_space=pl.ANY), vmem),
        scratch_shapes=[
            pltpu.VMEM((4, 4, 4, 2 * TILE, SKETCH), F32),
            pltpu.VMEM((3, 4, 6, 2, 88, SKETCH), F32),
            pltpu.VMEM((3, 6, 2, 88, SKETCH), F32),
            pltpu.VMEM((3, 6, 48, SKETCH), F32),
            pltpu.VMEM((CB_DEV * TILE, SKETCH), BF16),
            pltpu.VMEM((2,) + sq, F32),
            pltpu.VMEM((2,) + sq, F32),
            pltpu.VMEM((SKETCH, 2 * SKETCH), F32),
            pltpu.VMEM(sq, F32),
            pltpu.VMEM(sq, F32),
            pltpu.VMEM((2 * TILE, SKETCH), F32),
            pltpu.VMEM((2, 3) + part, F32),
            pltpu.VMEM((2, 8) + part, F32),
            pltpu.VMEM((2, 2, 4) + part, F32),
            pltpu.SemaphoreType.DMA((48,)),
            pltpu.SemaphoreType.DMA((48,)),
            pltpu.SemaphoreType.DMA((108,)),
            pltpu.SemaphoreType.DMA((108,)),
            pltpu.SemaphoreType.DMA((2, 21)),
            pltpu.SemaphoreType.DMA((2, 21)),
            pltpu.SemaphoreType.DMA((4,)),
        ],
        compiler_params=pltpu.CompilerParams(
            collective_id=0, has_side_effects=True, vmem_limit_bytes=26 << 20),
    )(pltpu.with_memory_space_constraint(split, pltpu.VMEM), pltpu.with_memory_space_constraint(w, pltpu.VMEM))


def on_device(tiles, tile_rows, tile_cols, tile_counts, block_order, sketch):
    split, w = local_pass(tiles, tile_rows, tile_cols, tile_counts, block_order, sketch)
    return exchange(split, w)


def solution(mesh):
    placed = (
        P(("gx", "gy"), None, None),
        P(("gx", "gy")),
        P(("gx", "gy")),
        P(("gx", "gy")),
        P(),
        P(),
    )
    return jax.shard_map(
        on_device,
        mesh=mesh,
        in_specs=placed,
        out_specs=(P(("gx", "gy"), None), P(("gx", "gy"), None)),
        check_vma=False,
    )
```

```python
import math

import jax
import jax.numpy as jnp
from jax import lax
from jax.experimental import pallas as pl
from jax.experimental.pallas import tpu as pltpu
from jax.sharding import PartitionSpec as P

TILE = 128
SKETCH = 128
GENES = 32768
CB_DEV = 64
BLOCKS = 256
SLOTS = 192
GROUP = 32
CHUNK = 32
F32 = jnp.float32
BF16 = jnp.bfloat16


def local_kernel(counts, rows_hbm, cols_hbm, order_hbm, tiles_hbm, sketch_hbm, split, w_out,
                 tiles, sketch, y_ref, place, rows, cols, order,
                 tile_sems, sketch_sems, index_sems):
    lists = ((rows_hbm, rows), (cols_hbm, cols), (order_hbm, order))
    index_copies = [pltpu.make_async_copy(a, b, index_sems.at[i]) for i, (a, b) in enumerate(lists)]
    for copy in index_copies:
        copy.start()
    w_ref = w_out.reshape(BLOCKS, TILE, SKETCH)
    n_tile = SLOTS // CHUNK
    n_sk = 4
    sk = GENES // n_sk

    def tile_copy(i):
        return pltpu.make_async_copy(
            tiles_hbm.at[pl.ds(i * CHUNK, CHUNK)], tiles.at[pl.ds(i * CHUNK, CHUNK)], tile_sems.at[i])

    def sketch_copy(i):
        return pltpu.make_async_copy(
            sketch_hbm.at[pl.ds(i * sk, sk)], sketch.at[pl.ds(i * sk, sk)], sketch_sems.at[i])

    for i in range(n_sk):
        sketch_copy(i).start()
    for i in range(n_tile):
        tile_copy(i).start()

    for copy in index_copies:
        copy.wait()
    live = counts[0]

    def invert(i, _):
        for u in range(8):
            place[order[i * 8 + u]] = i * 8 + u
        return 0
    lax.fori_loop(0, BLOCKS // 8, invert, 0)

    def clear_y(i, _):
        for u in range(4):
            y_ref[i * 4 + u] = jnp.zeros((TILE, SKETCH), F32)
        return 0
    lax.fori_loop(0, CB_DEV // 4, clear_y, 0)

    def clear_w(i, _):
        for u in range(4):
            w_ref[i * 4 + u] = jnp.zeros((TILE, SKETCH), F32)
        return 0
    lax.fori_loop(0, BLOCKS // 4, clear_w, 0)

    for i in range(n_sk):
        sketch_copy(i).wait()

    def cells(i):
        base = i * GROUP
        parts = []
        for u in range(GROUP):
            c = pl.multiple_of(cols[base + u] * TILE, TILE)
            p = jnp.dot(tiles[base + u], sketch[pl.ds(c, TILE), :], preferred_element_type=F32)
            parts.append(jnp.where(base + u < live, p, 0.0))
        for u in range(GROUP):
            r = rows[base + u]
            y_ref[r] = y_ref[r] + parts[u]

    def cell_body(i, _):
        @pl.when(i % (CHUNK // GROUP) == 0)
        def _():
            tile_copy(i // (CHUNK // GROUP)).wait()
        cells(i)
        return 0
    steps = (live + GROUP - 1) // GROUP
    lax.fori_loop(0, steps, cell_body, 0)

    def late(i, _):
        tile_copy(i).wait()
        return 0
    lax.fori_loop((live + CHUNK - 1) // CHUNK, n_tile, late, 0)

    def cut(i, _):
        for u in range(4):
            v = y_ref[i * 4 + u]
            hi = v.astype(BF16)
            split[i * 4 + u, :, :SKETCH] = hi
            split[i * 4 + u, :, SKETCH:] = (v - hi.astype(F32)).astype(BF16)
        return 0
    lax.fori_loop(0, CB_DEV // 4, cut, 0)

    def gene_body(i, _):
        base = i * GROUP
        parts = []
        for u in range(GROUP):
            r = rows[base + u]
            p = lax.dot_general(tiles[base + u], split[r], (((0,), (0,)), ((), ())),
                                preferred_element_type=F32)
            v = p[:, :SKETCH] + p[:, SKETCH:]
            parts.append(jnp.where(base + u < live, v, 0.0))
        for u in range(GROUP):
            o = place[cols[base + u]]
            w_ref[o] = w_ref[o] + parts[u]
        return 0
    lax.fori_loop(0, steps, gene_body, 0)


def local_pass(tiles, rows, cols, counts, order, sketch):
    hbm = [pltpu.with_memory_space_constraint(v, pltpu.HBM) for v in (rows, cols, order, tiles, sketch)]
    anyp = pl.BlockSpec(memory_space=pl.ANY)
    vmem = pl.BlockSpec(memory_space=pltpu.VMEM)
    return pl.pallas_call(
        local_kernel,
        name="local_pass",
        out_shape=(
            pltpu.VMEM((CB_DEV, TILE, 2 * SKETCH), BF16),
            pltpu.VMEM((4, 2, 4, 4, 2 * TILE, SKETCH), F32),
        ),
        in_specs=[pl.BlockSpec(memory_space=pltpu.SMEM)] + [anyp] * 5,
        out_specs=(vmem, vmem),
        scratch_shapes=[
            pltpu.VMEM((SLOTS, TILE, TILE), BF16),
            pltpu.VMEM((GENES, SKETCH), BF16),
            pltpu.VMEM((CB_DEV, TILE, SKETCH), F32),
            pltpu.SMEM((BLOCKS,), jnp.int32),
            pltpu.SMEM((SLOTS,), jnp.int32),
            pltpu.SMEM((SLOTS,), jnp.int32),
            pltpu.SMEM((BLOCKS,), jnp.int32),
            pltpu.SemaphoreType.DMA((SLOTS // CHUNK,)),
            pltpu.SemaphoreType.DMA((4,)),
            pltpu.SemaphoreType.DMA((4,)),
        ],
        compiler_params=pltpu.CompilerParams(vmem_limit_bytes=26 << 20),
    )(counts, *hbm)


PARTS = ((0, 88), (88, 88), (176, 80))
ORDERS = ((2, 1, 0), (1, 0, 2), (0, 2, 1))
ROUNDS = (2, 1, 3, 0)
TURN = (0, 1, 1, 0, 0, 1)
MESH = pl.DeviceIdType.MESH
HIGH = lax.Precision.HIGHEST


def cut_two(v):
    hi = v.astype(BF16)
    return hi, (v - hi.astype(F32)).astype(BF16)


WINDOW = 4


def factor_start(gram, work):
    work[:, :SKETCH] = gram[...]
    ri = lax.broadcasted_iota(jnp.int32, (SKETCH, SKETCH), 0)
    ci = lax.broadcasted_iota(jnp.int32, (SKETCH, SKETCH), 1)
    work[:, SKETCH:] = jnp.where(ri == ci, 1.0, 0.0)


def factor_steps(work, out, first, last):
    rows = 32
    down = lax.broadcasted_iota(jnp.int32, (rows, 1), 0)

    def lane(v, n):
        return jnp.broadcast_to(v[:, n:n + 1], (v.shape[0], SKETCH))

    def group(j, l0):
        tile = pl.ds(pl.multiple_of(j, 8), 8)
        lt = work[tile, :SKETCH]
        rt = work[tile, SKETCH:]
        left = [jnp.broadcast_to(lt[l0 + t:l0 + t + 1], (8, SKETCH)) for t in range(WINDOW)]
        right = [jnp.broadcast_to(rt[l0 + t:l0 + t + 1], (8, SKETCH)) for t in range(WINDOW)]
        e = {(s, t): lane(left[s], l0 + t) for s in range(WINDOW) for t in range(s, WINDOW)}
        w = {}
        inv = []
        for s in range(WINDOW):
            inv.append(1.0 / e[s, s])
            for t in range(s + 1, WINDOW):
                w[s, t] = e[s, t] * inv[s]
            for t in range(s + 1, WINDOW):
                for u in range(t, WINDOW):
                    e[t, u] = e[t, u] - w[s, t] * e[s, u]
                left[t] = left[t] - w[s, t] * left[s]
                right[t] = right[t] - w[s, t] * right[s]
        done = [right[t] * (1.0 / jnp.sqrt(e[t, t])) for t in range(WINDOW)]
        ql = [(left[t] * inv[t])[:1] for t in range(WINDOW)]
        qr = [(right[t] * inv[t])[:1] for t in range(WINDOW)]
        ww = {k: v[:1] for k, v in w.items()}
        for i in range(first * 8 // rows, SKETCH // rows):
            here = pl.ds(i * rows, rows)
            a = work[here, :SKETCH]
            b = work[here, SKETCH:]
            below = down + i * rows > j + l0 + WINDOW - 1
            c = [jnp.where(below, lane(a, l0 + t), 0.0) for t in range(WINDOW)]
            for t in range(1, WINDOW):
                for s in range(t):
                    c[t] = c[t] - c[s] * ww[s, t]
            for t in range(WINDOW):
                a = a - c[t] * ql[t]
                b = b - c[t] * qr[t]
            if l0 + WINDOW == 8:
                a = pltpu.roll(a, SKETCH - 8, 1)
            work[here, :SKETCH] = a
            work[here, SKETCH:] = b
        return done

    sub = lax.broadcasted_iota(jnp.int32, (8, 1), 0)

    def body(i, carry):
        done = []
        for l0 in range(0, 8, WINDOW):
            done += group(i * 8, l0)
        tile = done[0]
        for t in range(1, 8):
            tile = jnp.where(sub == t, done[t], tile)
        out[pl.ds(pl.multiple_of(i * 8, 8), 8), :] = tile
        return carry

    lax.fori_loop(first, last, body, 0)


def exchange_kernel(split, w, cell, zed, total2,
                    acc, box1, box2, box3, gram, total, work, inv1,
                    cur, first, slots,
                    in_send, in_recv, ring_send, ring_recv, sum_send, sum_recv):
    gx = lax.axis_index("gx")
    gy = lax.axis_index("gy")
    z, core = gx // 2, gx % 2
    y, x = gy // 4, gy % 4
    me = (z, y, x)

    def device(pos, c):
        return (pos[0] * 2 + c, pos[1] * 4 + pos[2])

    def around(axis, k):
        return (me[axis] + k + 4) % 4

    def moved(axis, k):
        pos = list(me)
        pos[axis] = around(axis, k)
        return pos

    near = [(dx, dc) for dx in range(4) for dc in range(2) if dx or dc]

    def near_device(dx, dc):
        return device(moved(2, dx), 1 - core if dc else core)

    partner = near_device(0, 1)
    barrier = pltpu.get_barrier_semaphore()
    peers = [near_device(dx, dc) for dx, dc in near]
    peers += [device(moved(a, k), core) for a in (0, 1) for k in (1, 2, 3)]
    for peer in peers:
        pl.semaphore_signal(barrier, inc=1, device_id=peer, device_id_type=MESH)
    pl.semaphore_wait(barrier, len(peers))

    sends = []

    def remote(src, dst, send, recv, peer):
        copy = pltpu.make_async_remote_copy(
            src_ref=src, dst_ref=dst, send_sem=send, recv_sem=recv,
            device_id=peer, device_id_type=MESH)
        copy.start()
        sends.append(copy)
        return copy

    def add(dst, src, lead):
        if lead:
            def body(i, carry):
                dst[i] = dst[i] + src[i]
                return carry
            lax.fori_loop(0, lead, body, 0)
        else:
            dst[...] = dst[...] + src[...]

    def place(p, ca, cb, cc, rows=None):
        idx = [None] * 3
        for d, v in zip(ORDERS[p], (ca, cb, cc)):
            idx[d] = v
        r0, nr = PARTS[p]
        if rows is not None:
            r0, nr = r0 + rows[0], rows[1]
        return tuple(idx) + (pl.ds(r0, nr),)

    def with_core(idx, c):
        return (idx[0], c) + tuple(idx[1:])

    pieces = {}

    def piece(k, q, p):
        n = (k * 4 + q) * 3 + p
        a, b = ORDERS[p][:2]
        idx = place(p, around(a, k), around(b, q), slice(None))
        pieces[k, q, p] = idx, remote(w.at[with_core(idx, 1 - core)], acc.at[idx],
                                      in_send.at[n], in_recv.at[n], partner)

    def merge(k, q, p):
        idx, copy = pieces[k, q, p]
        copy.wait_recv()
        add(acc.at[idx], w.at[with_core(idx, core)], 4)

    share = SKETCH // 8
    mine = pl.ds((x * 2 + core) * share, share)

    def sum_start(s):
        first[s, x * 2 + core] = gram[s, mine, :]
        out = []
        for dx, dc in near:
            n = dx * 2 + dc
            to = around(2, dx) * 2 + ((1 - core) if dc else core)
            out.append(remote(gram.at[s, pl.ds(to * share, share)], first.at[s, x * 2 + core],
                              sum_send.at[s, n], sum_recv.at[s, n], near_device(dx, dc)))
        return out

    def landed(copies):
        for copy in copies:
            copy.wait_recv()

    def sum_along(s, a, value):
        cur[s, a] = value
        slots[s, a, me[a]] = value
        out = []
        for k in (1, 2, 3):
            n = 7 + a * 3 + k
            out.append(remote(cur.at[s, a], slots.at[s, a, me[a]], sum_send.at[s, n], sum_recv.at[s, n],
                              device(moved(a, k), core)))
        return out

    def sum_first(s, copies):
        landed(copies)
        v = [first[s, n] for n in range(8)]
        return ((v[0] + v[1]) + (v[2] + v[3])) + ((v[4] + v[5]) + (v[6] + v[7]))

    def sum_next(s, a, copies):
        landed(copies)
        return (slots[s, a, 0] + slots[s, a, 1]) + (slots[s, a, 2] + slots[s, a, 3])

    def sum_spread(s, value):
        cur[s, 2] = value
        total[s, mine, :] = value
        out = []
        for dx, dc in near:
            n = 13 + dx * 2 + dc
            out.append(remote(cur.at[s, 2], total.at[s, mine], sum_send.at[s, n], sum_recv.at[s, n],
                              near_device(dx, dc)))
        return out

    ring = {}

    def half(h):
        return pl.ds(2 * h, 2)

    def view(phase, p, q, coord, h):
        a, b, c = ORDERS[p]
        if phase == 0:
            return acc.at[place(p, coord, around(b, q), half(h))]
        if phase == 1:
            return acc.at[place(p, me[a], coord, half(h))]
        return acc.at[place(p, me[a], me[b], coord, tail(p, h))]

    def tail(p, h):
        return (0, 48) if h == 0 else (48, PARTS[p][1] - 48)

    def box(phase, p, q, m, h):
        nr = PARTS[p][1]
        if phase == 0:
            return box1.at[p, q, m, :, pl.ds(0, nr)]
        if phase == 1:
            return box2.at[p, m, :, pl.ds(0, nr)]
        return box3.at[p, m, pl.ds(0, tail(p, h)[1])]

    def send(phase, p, q, m):
        axis = ORDERS[p][phase]
        sign = 1 if m % 2 == 0 else -1
        h = TURN[m]
        n = (p * 4 + q) * 6 + m if phase == 0 else 72 + (phase - 1) * 18 + p * 6 + m
        ring[phase, p, q, m] = remote(
            view(phase, p, q, around(axis, 2 if m < 2 else sign), h), box(phase, p, q, m, h),
            ring_send.at[n], ring_recv.at[n], device(moved(axis, sign), core))

    def relay(phase, p, q, m):
        axis = ORDERS[p][phase]
        sign = 1 if m == 0 else -1
        ring[phase, p, q, m].wait_recv()
        add(view(phase, p, q, around(axis, sign), m), box(phase, p, q, m, m), 0 if phase == 2 else 2)
        send(phase, p, q, 4 + m)

    def land(phase, p, q, m):
        ring[phase, p, q, m].wait_recv()
        add(view(phase, p, q, me[ORDERS[p][phase]], TURN[m]), box(phase, p, q, m, TURN[m]),
            0 if phase == 2 else 2)

    def open_round(q):
        for p in range(3):
            merge(2, q, p)
            send(0, p, q, 0)
            send(0, p, q, 1)
        for p in range(3):
            merge(1, q, p)
            send(0, p, q, 2)
            merge(3, q, p)
            send(0, p, q, 3)

    def relay_round(q):
        for p in range(3):
            relay(0, p, q, 0)
            relay(0, p, q, 1)

    def close_round(q):
        for p in range(3):
            merge(0, q, p)
        for m in (2, 3, 4, 5):
            for p in range(3):
                land(0, p, q, m)
        for p in range(3):
            if q == 2:
                send(1, p, 0, 0)
                send(1, p, 0, 1)
            elif q == 1:
                send(1, p, 0, 2)
            elif q == 3:
                send(1, p, 0, 3)
        if q in (1, 3):
            for p in range(3):
                relay(1, p, 0, 0 if q == 1 else 1)

    for k in ROUNDS:
        for p in range(3):
            piece(k, 2, p)

    def gram_body(i, g):
        v = split[pl.ds(i * 8, 8)].reshape(8 * TILE, 2 * SKETCH)
        return g + lax.dot_general(v, v, (((0,), (0,)), ((), ())), preferred_element_type=F32)
    g = lax.fori_loop(0, CB_DEV // 8, gram_body, jnp.zeros((2 * SKETCH, 2 * SKETCH), F32))
    gram[0] = (g[:SKETCH, :SKETCH] + g[SKETCH:, SKETCH:]) + (g[:SKETCH, SKETCH:] + g[SKETCH:, :SKETCH])
    copies = sum_start(0)
    for q in ROUNDS[1:]:
        for k in ROUNDS:
            for p in range(3):
                piece(k, q, p)

    open_round(2)
    copies = sum_along(0, 1, sum_first(0, copies))
    open_round(1)
    relay_round(2)
    copies = sum_along(0, 0, sum_next(0, 1, copies))
    open_round(3)
    relay_round(1)
    close_round(2)
    copies = sum_spread(0, sum_next(0, 0, copies))
    open_round(0)
    relay_round(3)
    close_round(1)
    landed(copies)
    factor_start(total.at[0], work)
    factor_steps(work, inv1, 0, 5)
    relay_round(0)
    factor_steps(work, inv1, 5, 10)
    close_round(3)
    factor_steps(work, inv1, 10, 16)
    close_round(0)
    for m in (2, 3, 4, 5):
        for p in range(3):
            land(1, p, 0, m)
    for m in range(4):
        for p in range(3):
            send(2, p, 0, m)
    lh, ll = cut_two(inv1[...] * math.sqrt(CB_DEV * TILE * 128))
    weights = jnp.concatenate(
        [jnp.concatenate([lh, lh], axis=1), jnp.concatenate([ll, jnp.zeros_like(ll)], axis=1)], axis=0)
    for p in range(3):
        relay(2, p, 0, 0)
        relay(2, p, 0, 1)
    for m in (2, 3, 4, 5):
        for p in range(3):
            land(2, p, 0, m)

    zv = lax.dot_general(acc[z, y, x], inv1[...], (((1,), (1,)), ((), ())),
                         precision=HIGH, preferred_element_type=F32)
    zed[...] = zv
    gram[1] = lax.dot_general(zv, zv, (((0,), (0,)), ((), ())), precision=HIGH, preferred_element_type=F32)

    def cells(n):
        def body(i, carry):
            v = split[pl.ds(i * 4, 4)].reshape(4 * TILE, 2 * SKETCH)
            o = lax.dot_general(v, weights, (((1,), (1,)), ((), ())), preferred_element_type=F32)
            cell[pl.ds(pl.multiple_of(i * 4 * TILE, 4 * TILE), 4 * TILE), :] = (
                o[:, :SKETCH] + o[:, SKETCH:]).astype(BF16)
            return carry
        lax.fori_loop(n * 4, n * 4 + 4, body, 0)

    copies = sum_start(1)
    cells(0)
    copies = sum_along(1, 1, sum_first(1, copies))
    cells(1)
    copies = sum_along(1, 0, sum_next(1, 1, copies))
    cells(2)
    copies = sum_spread(1, sum_next(1, 0, copies))
    cells(3)
    landed(copies)
    total2[...] = total[1]
    for copy in sends:
        copy.wait_send()


def finish_kernel(cell, zed, gram, cell_out, gene_out, work, inv2, out_sem):
    copy = pltpu.make_async_copy(cell, cell_out, out_sem.at[0])
    copy.start()
    factor_start(gram, work)
    for n in range(4):
        factor_steps(work, inv2, n * 4, n * 4 + 4)
    gene_out[...] = math.sqrt(GENES) * lax.dot_general(
        zed[...], inv2[...], (((1,), (1,)), ((), ())), precision=HIGH, preferred_element_type=F32)
    copy.wait()


def exchange(split, w):
    vmem = pl.BlockSpec(memory_space=pltpu.VMEM)
    sq = (SKETCH, SKETCH)
    part = (SKETCH // 8, SKETCH)
    return pl.pallas_call(
        exchange_kernel,
        name="exchange",
        out_shape=(
            pltpu.VMEM((CB_DEV * TILE, SKETCH), BF16),
            pltpu.VMEM((2 * TILE, SKETCH), F32),
            pltpu.VMEM(sq, F32),
        ),
        in_specs=[vmem, vmem],
        out_specs=(vmem, vmem, vmem),
        scratch_shapes=[
            pltpu.VMEM((4, 4, 4, 2 * TILE, SKETCH), F32),
            pltpu.VMEM((3, 4, 6, 2, 88, SKETCH), F32),
            pltpu.VMEM((3, 6, 2, 88, SKETCH), F32),
            pltpu.VMEM((3, 6, 48, SKETCH), F32),
            pltpu.VMEM((2,) + sq, F32),
            pltpu.VMEM((2,) + sq, F32),
            pltpu.VMEM((SKETCH, 2 * SKETCH), F32),
            pltpu.VMEM(sq, F32),
            pltpu.VMEM((2, 3) + part, F32),
            pltpu.VMEM((2, 8) + part, F32),
            pltpu.VMEM((2, 2, 4) + part, F32),
            pltpu.SemaphoreType.DMA((48,)),
            pltpu.SemaphoreType.DMA((48,)),
            pltpu.SemaphoreType.DMA((108,)),
            pltpu.SemaphoreType.DMA((108,)),
            pltpu.SemaphoreType.DMA((2, 21)),
            pltpu.SemaphoreType.DMA((2, 21)),
        ],
        compiler_params=pltpu.CompilerParams(
            collective_id=0, has_side_effects=True, vmem_limit_bytes=26 << 20),
    )(pltpu.with_memory_space_constraint(split, pltpu.VMEM), pltpu.with_memory_space_constraint(w, pltpu.VMEM))


def finish(cell, zed, gram):
    vmem = pl.BlockSpec(memory_space=pltpu.VMEM)
    held = [pltpu.with_memory_space_constraint(v, pltpu.VMEM) for v in (cell, zed, gram)]
    return pl.pallas_call(
        finish_kernel,
        name="finish",
        out_shape=(
            jax.ShapeDtypeStruct((CB_DEV * TILE, SKETCH), BF16),
            jax.ShapeDtypeStruct((2 * TILE, SKETCH), F32),
        ),
        in_specs=[vmem, vmem, vmem],
        out_specs=(pl.BlockSpec(memory_space=pl.ANY), vmem),
        scratch_shapes=[
            pltpu.VMEM((SKETCH, 2 * SKETCH), F32),
            pltpu.VMEM((SKETCH, SKETCH), F32),
            pltpu.SemaphoreType.DMA((1,)),
        ],
        compiler_params=pltpu.CompilerParams(vmem_limit_bytes=26 << 20),
    )(*held)


def on_device(tiles, tile_rows, tile_cols, tile_counts, block_order, sketch):
    split, w = local_pass(tiles, tile_rows, tile_cols, tile_counts, block_order, sketch)
    return finish(*exchange(split, w))


def solution(mesh):
    placed = (
        P(("gx", "gy"), None, None),
        P(("gx", "gy")),
        P(("gx", "gy")),
        P(("gx", "gy")),
        P(),
        P(),
    )
    return jax.shard_map(
        on_device,
        mesh=mesh,
        in_specs=placed,
        out_specs=(P(("gx", "gy"), None), P(("gx", "gy"), None)),
        check_vma=False,
    )
```

```python
import math

import jax
import jax.numpy as jnp
from jax import lax
from jax.experimental import pallas as pl
from jax.experimental.pallas import tpu as pltpu
from jax.sharding import PartitionSpec as P

TILE = 128
SKETCH = 128
GENES = 32768
CB_DEV = 64
BLOCKS = 256
SLOTS = 192
GROUP = 64
CHUNK = 64
F32 = jnp.float32
BF16 = jnp.bfloat16


def local_kernel(counts, rows_hbm, cols_hbm, order_hbm, tiles_hbm, sketch_hbm, split, w_out,
                 tiles, sketch, y_ref, place, rows, cols, order,
                 tile_sems, sketch_sems, index_sems):
    lists = ((rows_hbm, rows), (cols_hbm, cols), (order_hbm, order))
    index_copies = [pltpu.make_async_copy(a, b, index_sems.at[i]) for i, (a, b) in enumerate(lists)]
    for copy in index_copies:
        copy.start()
    w_ref = w_out.reshape(BLOCKS, TILE, SKETCH)
    n_tile = SLOTS // CHUNK
    n_sk = 4
    sk = GENES // n_sk

    def tile_copy(i):
        return pltpu.make_async_copy(
            tiles_hbm.at[pl.ds(i * CHUNK, CHUNK)], tiles.at[pl.ds(i * CHUNK, CHUNK)], tile_sems.at[i])

    def sketch_copy(i):
        return pltpu.make_async_copy(
            sketch_hbm.at[pl.ds(i * sk, sk)], sketch.at[pl.ds(i * sk, sk)], sketch_sems.at[i])

    for i in range(n_sk):
        sketch_copy(i).start()
    for i in range(n_tile):
        tile_copy(i).start()

    for copy in index_copies:
        copy.wait()
    live = counts[0]

    def invert(i, _):
        for u in range(8):
            place[order[i * 8 + u]] = i * 8 + u
        return 0
    lax.fori_loop(0, BLOCKS // 8, invert, 0)

    def clear_y(i, _):
        for u in range(4):
            y_ref[i * 4 + u] = jnp.zeros((TILE, SKETCH), F32)
        return 0
    lax.fori_loop(0, CB_DEV // 4, clear_y, 0)

    def clear_w(i, _):
        for u in range(4):
            w_ref[i * 4 + u] = jnp.zeros((TILE, SKETCH), F32)
        return 0
    lax.fori_loop(0, BLOCKS // 4, clear_w, 0)

    for i in range(n_sk):
        sketch_copy(i).wait()

    def cells(i):
        base = i * GROUP
        parts = []
        for u in range(GROUP):
            c = pl.multiple_of(cols[base + u] * TILE, TILE)
            p = jnp.dot(tiles[base + u], sketch[pl.ds(c, TILE), :], preferred_element_type=F32)
            parts.append(jnp.where(base + u < live, p, 0.0))
        for u in range(GROUP):
            r = rows[base + u]
            y_ref[r] = y_ref[r] + parts[u]

    def cell_body(i, _):
        @pl.when(i % (CHUNK // GROUP) == 0)
        def _():
            tile_copy(i // (CHUNK // GROUP)).wait()
        cells(i)
        return 0
    steps = (live + GROUP - 1) // GROUP
    lax.fori_loop(0, steps, cell_body, 0)

    def late(i, _):
        tile_copy(i).wait()
        return 0
    lax.fori_loop((live + CHUNK - 1) // CHUNK, n_tile, late, 0)

    def cut(i, _):
        for u in range(4):
            v = y_ref[i * 4 + u]
            hi = v.astype(BF16)
            split[i * 4 + u, :, :SKETCH] = hi
            split[i * 4 + u, :, SKETCH:] = (v - hi.astype(F32)).astype(BF16)
        return 0
    lax.fori_loop(0, CB_DEV // 4, cut, 0)

    def gene_body(i, _):
        base = i * GROUP
        parts = []
        for u in range(GROUP):
            r = rows[base + u]
            p = lax.dot_general(tiles[base + u], split[r], (((0,), (0,)), ((), ())),
                                preferred_element_type=F32)
            v = p[:, :SKETCH] + p[:, SKETCH:]
            parts.append(jnp.where(base + u < live, v, 0.0))
        for u in range(GROUP):
            o = place[cols[base + u]]
            w_ref[o] = w_ref[o] + parts[u]
        return 0
    lax.fori_loop(0, steps, gene_body, 0)


def local_pass(tiles, rows, cols, counts, order, sketch):
    hbm = [pltpu.with_memory_space_constraint(v, pltpu.HBM) for v in (rows, cols, order, tiles, sketch)]
    anyp = pl.BlockSpec(memory_space=pl.ANY)
    vmem = pl.BlockSpec(memory_space=pltpu.VMEM)
    return pl.pallas_call(
        local_kernel,
        name="local_pass",
        out_shape=(
            pltpu.VMEM((CB_DEV, TILE, 2 * SKETCH), BF16),
            pltpu.VMEM((4, 2, 4, 4, 2 * TILE, SKETCH), F32),
        ),
        in_specs=[pl.BlockSpec(memory_space=pltpu.SMEM)] + [anyp] * 5,
        out_specs=(vmem, vmem),
        scratch_shapes=[
            pltpu.VMEM((SLOTS, TILE, TILE), BF16),
            pltpu.VMEM((GENES, SKETCH), BF16),
            pltpu.VMEM((CB_DEV, TILE, SKETCH), F32),
            pltpu.SMEM((BLOCKS,), jnp.int32),
            pltpu.SMEM((SLOTS,), jnp.int32),
            pltpu.SMEM((SLOTS,), jnp.int32),
            pltpu.SMEM((BLOCKS,), jnp.int32),
            pltpu.SemaphoreType.DMA((SLOTS // CHUNK,)),
            pltpu.SemaphoreType.DMA((4,)),
            pltpu.SemaphoreType.DMA((4,)),
        ],
        compiler_params=pltpu.CompilerParams(vmem_limit_bytes=26 << 20),
    )(counts, *hbm)


PARTS = ((0, 88), (88, 88), (176, 80))
ORDERS = ((2, 1, 0), (1, 0, 2), (0, 2, 1))
ROUNDS = (2, 1, 3, 0)
TURN = (0, 1, 1, 0, 0, 1)
MESH = pl.DeviceIdType.MESH


def cut_two(v):
    hi = v.astype(BF16)
    return hi, (v - hi.astype(F32)).astype(BF16)


WINDOW = 4


def split_weights(inverse):
    hi, lo = cut_two(inverse)
    return jnp.concatenate(
        [jnp.concatenate([hi, hi], axis=1), jnp.concatenate([lo, jnp.zeros_like(lo)], axis=1)], axis=0)


def split_dot(terms, weights):
    o = lax.dot_general(terms, weights, (((1,), (1,)), ((), ())), preferred_element_type=F32)
    return o[:, :SKETCH] + o[:, SKETCH:]


def split_gram(terms, g):
    g = g + lax.dot_general(terms, terms, (((0,), (0,)), ((), ())), preferred_element_type=F32)
    return g


def fold(g):
    return (g[:SKETCH, :SKETCH] + g[SKETCH:, SKETCH:]) + (g[:SKETCH, SKETCH:] + g[SKETCH:, :SKETCH])


def factor_start(gram, work):
    work[:, :SKETCH] = gram[...]
    ri = lax.broadcasted_iota(jnp.int32, (SKETCH, SKETCH), 0)
    ci = lax.broadcasted_iota(jnp.int32, (SKETCH, SKETCH), 1)
    work[:, SKETCH:] = jnp.where(ri == ci, 1.0, 0.0)


def factor_steps(work, out, first, last):
    rows = 32
    down = lax.broadcasted_iota(jnp.int32, (rows, 1), 0)

    def lane(v, n):
        return jnp.broadcast_to(v[:, n:n + 1], (v.shape[0], SKETCH))

    def group(j, l0):
        tile = pl.ds(pl.multiple_of(j, 8), 8)
        lt = work[tile, :SKETCH]
        rt = work[tile, SKETCH:]
        left = [jnp.broadcast_to(lt[l0 + t:l0 + t + 1], (8, SKETCH)) for t in range(WINDOW)]
        right = [jnp.broadcast_to(rt[l0 + t:l0 + t + 1], (8, SKETCH)) for t in range(WINDOW)]
        e = {(s, t): lane(left[s], l0 + t) for s in range(WINDOW) for t in range(s, WINDOW)}
        w = {}
        inv = []
        for s in range(WINDOW):
            inv.append(1.0 / e[s, s])
            for t in range(s + 1, WINDOW):
                w[s, t] = e[s, t] * inv[s]
            for t in range(s + 1, WINDOW):
                for u in range(t, WINDOW):
                    e[t, u] = e[t, u] - w[s, t] * e[s, u]
                left[t] = left[t] - w[s, t] * left[s]
                right[t] = right[t] - w[s, t] * right[s]
        done = [right[t] * (1.0 / jnp.sqrt(e[t, t])) for t in range(WINDOW)]
        ql = [(left[t] * inv[t])[:1] for t in range(WINDOW)]
        qr = [(right[t] * inv[t])[:1] for t in range(WINDOW)]
        ww = {k: v[:1] for k, v in w.items()}
        for i in range(first * 8 // rows, SKETCH // rows):
            here = pl.ds(i * rows, rows)
            a = work[here, :SKETCH]
            b = work[here, SKETCH:]
            below = down + i * rows > j + l0 + WINDOW - 1
            c = [jnp.where(below, lane(a, l0 + t), 0.0) for t in range(WINDOW)]
            for t in range(1, WINDOW):
                for s in range(t):
                    c[t] = c[t] - c[s] * ww[s, t]
            for t in range(WINDOW):
                a = a - c[t] * ql[t]
                b = b - c[t] * qr[t]
            if l0 + WINDOW == 8:
                a = pltpu.roll(a, SKETCH - 8, 1)
            work[here, :SKETCH] = a
            work[here, SKETCH:] = b
        return done

    sub = lax.broadcasted_iota(jnp.int32, (8, 1), 0)

    def body(i, carry):
        done = []
        for l0 in range(0, 8, WINDOW):
            done += group(i * 8, l0)
        tile = done[0]
        for t in range(1, 8):
            tile = jnp.where(sub == t, done[t], tile)
        out[pl.ds(pl.multiple_of(i * 8, 8), 8), :] = tile
        return carry

    lax.fori_loop(first, last, body, 0)


def exchange_kernel(split, w, cell, zed, total2,
                    acc, box1, box2, box3, gram, total, work, inv1,
                    cur, first, slots,
                    in_send, in_recv, ring_send, ring_recv, sum_send, sum_recv):
    gx = lax.axis_index("gx")
    gy = lax.axis_index("gy")
    z, core = gx // 2, gx % 2
    y, x = gy // 4, gy % 4
    me = (z, y, x)

    def device(pos, c):
        return (pos[0] * 2 + c, pos[1] * 4 + pos[2])

    def around(axis, k):
        return (me[axis] + k + 4) % 4

    def moved(axis, k):
        pos = list(me)
        pos[axis] = around(axis, k)
        return pos

    near = [(dx, dc) for dx in range(4) for dc in range(2) if dx or dc]

    def near_device(dx, dc):
        return device(moved(2, dx), 1 - core if dc else core)

    partner = near_device(0, 1)
    barrier = pltpu.get_barrier_semaphore()
    peers = [near_device(dx, dc) for dx, dc in near]
    peers += [device(moved(a, k), core) for a in (0, 1) for k in (1, 2, 3)]
    for peer in peers:
        pl.semaphore_signal(barrier, inc=1, device_id=peer, device_id_type=MESH)
    pl.semaphore_wait(barrier, len(peers))

    scale = math.sqrt(CB_DEV * TILE * 128)
    sends = []

    def remote(src, dst, send, recv, peer):
        copy = pltpu.make_async_remote_copy(
            src_ref=src, dst_ref=dst, send_sem=send, recv_sem=recv,
            device_id=peer, device_id_type=MESH)
        copy.start()
        sends.append(copy)
        return copy

    def add(dst, src, lead):
        def body(i, carry):
            dst[i] = dst[i] + src[i]
            return carry
        lax.fori_loop(0, lead, body, 0)

    def place(p, ca, cb, cc):
        idx = [None] * 3
        for d, v in zip(ORDERS[p], (ca, cb, cc)):
            idx[d] = v
        r0, nr = PARTS[p]
        return tuple(idx) + (pl.ds(r0, nr),)

    def with_core(idx, c):
        return (idx[0], c) + tuple(idx[1:])

    pieces = {}

    def piece(k, q, p):
        n = (k * 4 + q) * 3 + p
        a, b = ORDERS[p][:2]
        idx = place(p, around(a, k), around(b, q), slice(None))
        pieces[k, q, p] = idx, remote(w.at[with_core(idx, 1 - core)], acc.at[idx],
                                      in_send.at[n], in_recv.at[n], partner)

    def merge(k, q, p):
        idx, copy = pieces[k, q, p]
        copy.wait_recv()
        add(acc.at[idx], w.at[with_core(idx, core)], 4)

    share = SKETCH // 8
    mine = pl.ds((x * 2 + core) * share, share)

    def sum_start(s):
        first[s, x * 2 + core] = gram[s, mine, :]
        out = []
        for dx, dc in near:
            n = dx * 2 + dc
            to = around(2, dx) * 2 + ((1 - core) if dc else core)
            out.append(remote(gram.at[s, pl.ds(to * share, share)], first.at[s, x * 2 + core],
                              sum_send.at[s, n], sum_recv.at[s, n], near_device(dx, dc)))
        return out

    def landed(copies):
        for copy in copies:
            copy.wait_recv()

    def sum_along(s, a, value):
        cur[s, a] = value
        slots[s, a, me[a]] = value
        out = []
        for k in (1, 2, 3):
            n = 7 + a * 3 + k
            out.append(remote(cur.at[s, a], slots.at[s, a, me[a]], sum_send.at[s, n], sum_recv.at[s, n],
                              device(moved(a, k), core)))
        return out

    def sum_first(s, copies):
        landed(copies)
        v = [first[s, n] for n in range(8)]
        return ((v[0] + v[1]) + (v[2] + v[3])) + ((v[4] + v[5]) + (v[6] + v[7]))

    def sum_next(s, a, copies):
        landed(copies)
        return (slots[s, a, 0] + slots[s, a, 1]) + (slots[s, a, 2] + slots[s, a, 3])

    def sum_spread(s, value):
        cur[s, 2] = value
        total[s, mine, :] = value
        out = []
        for dx, dc in near:
            n = 13 + dx * 2 + dc
            out.append(remote(cur.at[s, 2], total.at[s, mine], sum_send.at[s, n], sum_recv.at[s, n],
                              near_device(dx, dc)))
        return out

    ring = {}

    def half(h):
        return pl.ds(2 * h, 2)

    def view(phase, p, q, coord, h):
        a, b, c = ORDERS[p]
        if phase == 0:
            return acc.at[place(p, coord, around(b, q), half(h))]
        return acc.at[place(p, me[a], coord, half(h))]

    def box(phase, p, q, m, h):
        nr = PARTS[p][1]
        if phase == 0:
            return box1.at[p, q, m, :, pl.ds(0, nr)]
        return box2.at[p, m, :, pl.ds(0, nr)]

    def send(phase, p, q, m):
        axis = ORDERS[p][phase]
        sign = 1 if m % 2 == 0 else -1
        h = TURN[m]
        n = (p * 4 + q) * 6 + m if phase == 0 else 72 + (phase - 1) * 18 + p * 6 + m
        ring[phase, p, q, m] = remote(
            view(phase, p, q, around(axis, 2 if m < 2 else sign), h), box(phase, p, q, m, h),
            ring_send.at[n], ring_recv.at[n], device(moved(axis, sign), core))

    def relay(phase, p, q, m):
        axis = ORDERS[p][phase]
        sign = 1 if m == 0 else -1
        ring[phase, p, q, m].wait_recv()
        add(view(phase, p, q, around(axis, sign), m), box(phase, p, q, m, m), 2)
        send(phase, p, q, 4 + m)

    def land(phase, p, q, m):
        ring[phase, p, q, m].wait_recv()
        add(view(phase, p, q, me[ORDERS[p][phase]], TURN[m]), box(phase, p, q, m, TURN[m]), 2)

    def open_far(q):
        for p in range(3):
            merge(2, q, p)
            send(0, p, q, 0)
            send(0, p, q, 1)

    def open_near(q):
        for p in range(3):
            merge(1, q, p)
            send(0, p, q, 2)
            merge(3, q, p)
            send(0, p, q, 3)

    def open_round(q):
        open_far(q)
        open_near(q)

    def relay_round(q):
        for p in range(3):
            relay(0, p, q, 0)
            relay(0, p, q, 1)

    def close_round(q):
        for p in range(3):
            merge(0, q, p)
        for m in (2, 3, 4, 5):
            for p in range(3):
                land(0, p, q, m)
        for p in range(3):
            if q == 2:
                send(1, p, 0, 0)
                send(1, p, 0, 1)
            elif q == 1:
                send(1, p, 0, 2)
            elif q == 3:
                send(1, p, 0, 3)
        if q in (1, 3):
            for p in range(3):
                relay(1, p, 0, 0 if q == 1 else 1)

    for k in ROUNDS:
        for p in range(3):
            piece(k, 2, p)

    open_far(2)

    def gram_body(i, g):
        v = split[pl.ds(i * 8, 8)].reshape(8 * TILE, 2 * SKETCH)
        return split_gram(v, g)
    g = lax.fori_loop(0, CB_DEV // 8, gram_body, jnp.zeros((2 * SKETCH, 2 * SKETCH), F32))
    gram[0] = fold(g)
    copies = sum_start(0)
    for q in ROUNDS[1:]:
        for k in ROUNDS:
            for p in range(3):
                piece(k, q, p)

    open_near(2)
    copies = sum_along(0, 1, sum_first(0, copies))
    open_round(1)
    relay_round(2)
    copies = sum_along(0, 0, sum_next(0, 1, copies))
    open_round(3)
    relay_round(1)
    close_round(2)
    copies = sum_spread(0, sum_next(0, 0, copies))
    open_round(0)
    relay_round(3)
    close_round(1)
    landed(copies)
    factor_start(total.at[0], work)
    factor_steps(work, inv1, 0, 5)
    relay_round(0)
    factor_steps(work, inv1, 5, 10)
    close_round(3)
    factor_steps(work, inv1, 10, 16)
    close_round(0)
    for m in (2, 3, 4, 5):
        for p in range(3):
            land(1, p, 0, m)
    last = {}
    for k in (2, 1, 3):
        for p in range(3):
            a, b, c = ORDERS[p]
            n = 90 + p * 3 + k - 1
            last[p, k] = remote(acc.at[place(p, me[a], me[b], around(c, k))],
                                box3.at[p, k - 1, pl.ds(0, PARTS[p][1])],
                                ring_send.at[n], ring_recv.at[n], device(moved(c, k), core))
    weights = split_weights(inv1[...] * scale)
    for p in range(3):
        a, b, c = ORDERS[p]
        nr = PARTS[p][1]
        for k in (1, 3, 2):
            last[p, k].wait_recv()
        own = acc.at[place(p, me[a], me[b], me[c])]
        own[...] = (own[...] + box3[p, 0, :nr]) + (box3[p, 1, :nr] + box3[p, 2, :nr])

    zv = split_dot(jnp.concatenate(cut_two(acc[z, y, x]), axis=1), weights) * (1.0 / scale)
    zv = jnp.concatenate(cut_two(zv), axis=1)
    zed[...] = zv
    gram[1] = fold(split_gram(zv, jnp.zeros((2 * SKETCH, 2 * SKETCH), F32)))

    def cells(n):
        def body(i, carry):
            v = split[pl.ds(i * 4, 4)].reshape(4 * TILE, 2 * SKETCH)
            cell[pl.ds(pl.multiple_of(i * 4 * TILE, 4 * TILE), 4 * TILE), :] = split_dot(v, weights).astype(BF16)
            return carry
        lax.fori_loop(n * 4, n * 4 + 4, body, 0)

    copies = sum_start(1)
    cells(0)
    copies = sum_along(1, 1, sum_first(1, copies))
    cells(1)
    copies = sum_along(1, 0, sum_next(1, 1, copies))
    cells(2)
    copies = sum_spread(1, sum_next(1, 0, copies))
    cells(3)
    landed(copies)
    total2[...] = total[1]
    for copy in sends:
        copy.wait_send()


def finish_kernel(cell, zed, gram, cell_out, gene_out, work, inv2, out_sem):
    copy = pltpu.make_async_copy(cell, cell_out, out_sem.at[0])
    copy.start()
    factor_start(gram, work)
    for n in range(4):
        factor_steps(work, inv2, n * 4, n * 4 + 4)
    gene_out[...] = split_dot(zed[...], split_weights(inv2[...] * math.sqrt(GENES)))
    copy.wait()


def exchange(split, w):
    vmem = pl.BlockSpec(memory_space=pltpu.VMEM)
    sq = (SKETCH, SKETCH)
    part = (SKETCH // 8, SKETCH)
    return pl.pallas_call(
        exchange_kernel,
        name="exchange",
        out_shape=(
            pltpu.VMEM((CB_DEV * TILE, SKETCH), BF16),
            pltpu.VMEM((2 * TILE, 2 * SKETCH), BF16),
            pltpu.VMEM(sq, F32),
        ),
        in_specs=[vmem, vmem],
        out_specs=(vmem, vmem, vmem),
        scratch_shapes=[
            pltpu.VMEM((4, 4, 4, 2 * TILE, SKETCH), F32),
            pltpu.VMEM((3, 4, 6, 2, 88, SKETCH), F32),
            pltpu.VMEM((3, 6, 2, 88, SKETCH), F32),
            pltpu.VMEM((3, 3, 88, SKETCH), F32),
            pltpu.VMEM((2,) + sq, F32),
            pltpu.VMEM((2,) + sq, F32),
            pltpu.VMEM((SKETCH, 2 * SKETCH), F32),
            pltpu.VMEM(sq, F32),
            pltpu.VMEM((2, 3) + part, F32),
            pltpu.VMEM((2, 8) + part, F32),
            pltpu.VMEM((2, 2, 4) + part, F32),
            pltpu.SemaphoreType.DMA((48,)),
            pltpu.SemaphoreType.DMA((48,)),
            pltpu.SemaphoreType.DMA((99,)),
            pltpu.SemaphoreType.DMA((99,)),
            pltpu.SemaphoreType.DMA((2, 21)),
            pltpu.SemaphoreType.DMA((2, 21)),
        ],
        compiler_params=pltpu.CompilerParams(
            collective_id=0, has_side_effects=True, vmem_limit_bytes=26 << 20),
    )(pltpu.with_memory_space_constraint(split, pltpu.VMEM), pltpu.with_memory_space_constraint(w, pltpu.VMEM))


def finish(cell, zed, gram):
    vmem = pl.BlockSpec(memory_space=pltpu.VMEM)
    held = [pltpu.with_memory_space_constraint(v, pltpu.VMEM) for v in (cell, zed, gram)]
    return pl.pallas_call(
        finish_kernel,
        name="finish",
        out_shape=(
            jax.ShapeDtypeStruct((CB_DEV * TILE, SKETCH), BF16),
            jax.ShapeDtypeStruct((2 * TILE, SKETCH), F32),
        ),
        in_specs=[vmem, vmem, vmem],
        out_specs=(pl.BlockSpec(memory_space=pl.ANY), vmem),
        scratch_shapes=[
            pltpu.VMEM((SKETCH, 2 * SKETCH), F32),
            pltpu.VMEM((SKETCH, SKETCH), F32),
            pltpu.SemaphoreType.DMA((1,)),
        ],
        compiler_params=pltpu.CompilerParams(vmem_limit_bytes=26 << 20),
    )(*held)


def on_device(tiles, tile_rows, tile_cols, tile_counts, block_order, sketch):
    split, w = local_pass(tiles, tile_rows, tile_cols, tile_counts, block_order, sketch)
    return finish(*exchange(split, w))


def solution(mesh):
    placed = (
        P(("gx", "gy"), None, None),
        P(("gx", "gy")),
        P(("gx", "gy")),
        P(("gx", "gy")),
        P(),
        P(),
    )
    return jax.shard_map(
        on_device,
        mesh=mesh,
        in_specs=placed,
        out_specs=(P(("gx", "gy"), None), P(("gx", "gy"), None)),
        check_vma=False,
    )
```

```python
import math

import jax
import jax.numpy as jnp
from jax import lax
from jax.experimental import pallas as pl
from jax.experimental.pallas import tpu as pltpu
from jax.sharding import PartitionSpec as P

TILE = 128
SKETCH = 128
GENES = 32768
CB_DEV = 64
BLOCKS = 256
SLOTS = 192
GROUP = 64
CHUNK = 64
F32 = jnp.float32
BF16 = jnp.bfloat16


def local_kernel(counts, rows_hbm, cols_hbm, order_hbm, tiles_hbm, sketch_hbm, split, w_out,
                 tiles, sketch, y_ref, place, rows, cols, order,
                 tile_sems, sketch_sems, index_sems):
    lists = ((rows_hbm, rows), (cols_hbm, cols), (order_hbm, order))
    index_copies = [pltpu.make_async_copy(a, b, index_sems.at[i]) for i, (a, b) in enumerate(lists)]
    for copy in index_copies:
        copy.start()
    w_ref = w_out.reshape(BLOCKS, TILE, SKETCH)
    n_tile = SLOTS // CHUNK
    n_sk = 4
    sk = GENES // n_sk

    def tile_copy(i):
        return pltpu.make_async_copy(
            tiles_hbm.at[pl.ds(i * CHUNK, CHUNK)], tiles.at[pl.ds(i * CHUNK, CHUNK)], tile_sems.at[i])

    def sketch_copy(i):
        return pltpu.make_async_copy(
            sketch_hbm.at[pl.ds(i * sk, sk)], sketch.at[pl.ds(i * sk, sk)], sketch_sems.at[i])

    for i in range(n_sk):
        sketch_copy(i).start()
    for i in range(n_tile):
        tile_copy(i).start()

    for copy in index_copies:
        copy.wait()
    live = counts[0]

    def invert(i, _):
        for u in range(8):
            place[order[i * 8 + u]] = i * 8 + u
        return 0
    lax.fori_loop(0, BLOCKS // 8, invert, 0)

    def clear_y(i, _):
        for u in range(4):
            y_ref[i * 4 + u] = jnp.zeros((TILE, SKETCH), F32)
        return 0
    lax.fori_loop(0, CB_DEV // 4, clear_y, 0)

    def clear_w(i, _):
        for u in range(4):
            w_ref[i * 4 + u] = jnp.zeros((TILE, SKETCH), F32)
        return 0
    lax.fori_loop(0, BLOCKS // 4, clear_w, 0)

    for i in range(n_sk):
        sketch_copy(i).wait()

    def cells(i):
        base = i * GROUP
        parts = []
        for u in range(GROUP):
            c = pl.multiple_of(cols[base + u] * TILE, TILE)
            p = jnp.dot(tiles[base + u], sketch[pl.ds(c, TILE), :], preferred_element_type=F32)
            parts.append(jnp.where(base + u < live, p, 0.0))
        for u in range(GROUP):
            r = rows[base + u]
            y_ref[r] = y_ref[r] + parts[u]

    def cell_body(i, _):
        @pl.when(i % (CHUNK // GROUP) == 0)
        def _():
            tile_copy(i // (CHUNK // GROUP)).wait()
        cells(i)
        return 0
    steps = (live + GROUP - 1) // GROUP
    lax.fori_loop(0, steps, cell_body, 0)

    def late(i, _):
        tile_copy(i).wait()
        return 0
    lax.fori_loop((live + CHUNK - 1) // CHUNK, n_tile, late, 0)

    def cut(i, _):
        for u in range(4):
            v = y_ref[i * 4 + u]
            hi = v.astype(BF16)
            split[i * 4 + u, :, :SKETCH] = hi
            split[i * 4 + u, :, SKETCH:] = (v - hi.astype(F32)).astype(BF16)
        return 0
    lax.fori_loop(0, CB_DEV // 4, cut, 0)

    def gene_body(i, _):
        base = i * GROUP
        parts = []
        for u in range(GROUP):
            r = rows[base + u]
            p = lax.dot_general(tiles[base + u], split[r], (((0,), (0,)), ((), ())),
                                preferred_element_type=F32)
            v = p[:, :SKETCH] + p[:, SKETCH:]
            parts.append(jnp.where(base + u < live, v, 0.0))
        for u in range(GROUP):
            o = place[cols[base + u]]
            w_ref[o] = w_ref[o] + parts[u]
        return 0
    lax.fori_loop(0, steps, gene_body, 0)


def local_pass(tiles, rows, cols, counts, order, sketch):
    hbm = [pltpu.with_memory_space_constraint(v, pltpu.HBM) for v in (rows, cols, order, tiles, sketch)]
    anyp = pl.BlockSpec(memory_space=pl.ANY)
    vmem = pl.BlockSpec(memory_space=pltpu.VMEM)
    return pl.pallas_call(
        local_kernel,
        name="local_pass",
        out_shape=(
            pltpu.VMEM((CB_DEV, TILE, 2 * SKETCH), BF16),
            pltpu.VMEM((4, 2, 4, 4, 2 * TILE, SKETCH), F32),
        ),
        in_specs=[pl.BlockSpec(memory_space=pltpu.SMEM)] + [anyp] * 5,
        out_specs=(vmem, vmem),
        scratch_shapes=[
            pltpu.VMEM((SLOTS, TILE, TILE), BF16),
            pltpu.VMEM((GENES, SKETCH), BF16),
            pltpu.VMEM((CB_DEV, TILE, SKETCH), F32),
            pltpu.SMEM((BLOCKS,), jnp.int32),
            pltpu.SMEM((SLOTS,), jnp.int32),
            pltpu.SMEM((SLOTS,), jnp.int32),
            pltpu.SMEM((BLOCKS,), jnp.int32),
            pltpu.SemaphoreType.DMA((SLOTS // CHUNK,)),
            pltpu.SemaphoreType.DMA((4,)),
            pltpu.SemaphoreType.DMA((4,)),
        ],
        compiler_params=pltpu.CompilerParams(vmem_limit_bytes=26 << 20),
    )(counts, *hbm)


PARTS = ((0, 88), (88, 88), (176, 80))
ORDERS = ((2, 1, 0), (1, 0, 2), (0, 2, 1))
ROUNDS = (2, 1, 3, 0)
TURN = (0, 1, 1, 0, 0, 1)
MESH = pl.DeviceIdType.MESH


def cut_two(v):
    hi = v.astype(BF16)
    return hi, (v - hi.astype(F32)).astype(BF16)


WINDOW = 4


def split_weights(inverse):
    hi, lo = cut_two(inverse)
    return jnp.concatenate(
        [jnp.concatenate([hi, hi], axis=1), jnp.concatenate([lo, jnp.zeros_like(lo)], axis=1)], axis=0)


def split_dot(terms, weights):
    o = lax.dot_general(terms, weights, (((1,), (1,)), ((), ())), preferred_element_type=F32)
    return o[:, :SKETCH] + o[:, SKETCH:]


def split_gram(terms, g):
    g = g + lax.dot_general(terms, terms, (((0,), (0,)), ((), ())), preferred_element_type=F32)
    return g


def fold(g):
    return (g[:SKETCH, :SKETCH] + g[SKETCH:, SKETCH:]) + (g[:SKETCH, SKETCH:] + g[SKETCH:, :SKETCH])


def factor_start(gram, work):
    work[:, :SKETCH] = gram[...]
    ri = lax.broadcasted_iota(jnp.int32, (SKETCH, SKETCH), 0)
    ci = lax.broadcasted_iota(jnp.int32, (SKETCH, SKETCH), 1)
    work[:, SKETCH:] = jnp.where(ri == ci, 1.0, 0.0)


def factor_steps(work, out, first, last):
    rows = 32
    down = lax.broadcasted_iota(jnp.int32, (rows, 1), 0)

    def lane(v, n):
        return jnp.broadcast_to(v[:, n:n + 1], (v.shape[0], SKETCH))

    def group(j, l0):
        tile = pl.ds(pl.multiple_of(j, 8), 8)
        lt = work[tile, :SKETCH]
        rt = work[tile, SKETCH:]
        left = [jnp.broadcast_to(lt[l0 + t:l0 + t + 1], (8, SKETCH)) for t in range(WINDOW)]
        right = [jnp.broadcast_to(rt[l0 + t:l0 + t + 1], (8, SKETCH)) for t in range(WINDOW)]
        e = {(s, t): lane(left[s], l0 + t) for s in range(WINDOW) for t in range(s, WINDOW)}
        w = {}
        inv = []
        for s in range(WINDOW):
            inv.append(1.0 / e[s, s])
            for t in range(s + 1, WINDOW):
                w[s, t] = e[s, t] * inv[s]
            for t in range(s + 1, WINDOW):
                for u in range(t, WINDOW):
                    e[t, u] = e[t, u] - w[s, t] * e[s, u]
                left[t] = left[t] - w[s, t] * left[s]
                right[t] = right[t] - w[s, t] * right[s]
        done = [right[t] * (1.0 / jnp.sqrt(e[t, t])) for t in range(WINDOW)]
        ql = [(left[t] * inv[t])[:1] for t in range(WINDOW)]
        qr = [(right[t] * inv[t])[:1] for t in range(WINDOW)]
        ww = {k: v[:1] for k, v in w.items()}
        for i in range(first * 8 // rows, SKETCH // rows):
            here = pl.ds(i * rows, rows)
            a = work[here, :SKETCH]
            b = work[here, SKETCH:]
            below = down + i * rows > j + l0 + WINDOW - 1
            c = [jnp.where(below, lane(a, l0 + t), 0.0) for t in range(WINDOW)]
            for t in range(1, WINDOW):
                for s in range(t):
                    c[t] = c[t] - c[s] * ww[s, t]
            for t in range(WINDOW):
                a = a - c[t] * ql[t]
                b = b - c[t] * qr[t]
            if l0 + WINDOW == 8:
                a = pltpu.roll(a, SKETCH - 8, 1)
            work[here, :SKETCH] = a
            work[here, SKETCH:] = b
        return done

    sub = lax.broadcasted_iota(jnp.int32, (8, 1), 0)

    def body(i, carry):
        done = []
        for l0 in range(0, 8, WINDOW):
            done += group(i * 8, l0)
        tile = done[0]
        for t in range(1, 8):
            tile = jnp.where(sub == t, done[t], tile)
        out[pl.ds(pl.multiple_of(i * 8, 8), 8), :] = tile
        return carry

    lax.fori_loop(first, last, body, 0)


def exchange_kernel(split, w, cell, zed, total2,
                    acc, box1, box2, box3, gram, total, work, inv1,
                    cur, first, slots,
                    in_send, in_recv, ring_send, ring_recv, sum_send, sum_recv):
    gx = lax.axis_index("gx")
    gy = lax.axis_index("gy")
    z, core = gx // 2, gx % 2
    y, x = gy // 4, gy % 4
    me = (z, y, x)

    def device(pos, c):
        return (pos[0] * 2 + c, pos[1] * 4 + pos[2])

    def around(axis, k):
        return (me[axis] + k + 4) % 4

    def moved(axis, k):
        pos = list(me)
        pos[axis] = around(axis, k)
        return pos

    near = [(dx, dc) for dx in range(4) for dc in range(2) if dx or dc]

    def near_device(dx, dc):
        return device(moved(2, dx), 1 - core if dc else core)

    partner = near_device(0, 1)
    barrier = pltpu.get_barrier_semaphore()
    peers = [near_device(dx, dc) for dx, dc in near]
    peers += [device(moved(a, k), core) for a in (0, 1) for k in (1, 2, 3)]
    for peer in peers:
        pl.semaphore_signal(barrier, inc=1, device_id=peer, device_id_type=MESH)
    pl.semaphore_wait(barrier, len(peers))

    scale = math.sqrt(CB_DEV * TILE * 128)
    sends = []

    def remote(src, dst, send, recv, peer):
        copy = pltpu.make_async_remote_copy(
            src_ref=src, dst_ref=dst, send_sem=send, recv_sem=recv,
            device_id=peer, device_id_type=MESH)
        copy.start()
        sends.append(copy)
        return copy

    def add(dst, src, lead):
        def body(i, carry):
            dst[i] = dst[i] + src[i]
            return carry
        lax.fori_loop(0, lead, body, 0)

    def place(p, ca, cb, cc):
        idx = [None] * 3
        for d, v in zip(ORDERS[p], (ca, cb, cc)):
            idx[d] = v
        r0, nr = PARTS[p]
        return tuple(idx) + (pl.ds(r0, nr),)

    def with_core(idx, c):
        return (idx[0], c) + tuple(idx[1:])

    pieces = {}

    def piece(k, q, p):
        n = (k * 4 + q) * 3 + p
        a, b = ORDERS[p][:2]
        idx = place(p, around(a, k), around(b, q), slice(None))
        pieces[k, q, p] = idx, remote(w.at[with_core(idx, 1 - core)], acc.at[idx],
                                      in_send.at[n], in_recv.at[n], partner)

    def merge(k, q, p):
        idx, copy = pieces[k, q, p]
        copy.wait_recv()
        add(acc.at[idx], w.at[with_core(idx, core)], 4)

    share = SKETCH // 8
    mine = pl.ds((x * 2 + core) * share, share)

    def sum_start(s):
        first[s, x * 2 + core] = gram[s, mine, :]
        out = []
        for dx, dc in near:
            n = dx * 2 + dc
            to = around(2, dx) * 2 + ((1 - core) if dc else core)
            out.append(remote(gram.at[s, pl.ds(to * share, share)], first.at[s, x * 2 + core],
                              sum_send.at[s, n], sum_recv.at[s, n], near_device(dx, dc)))
        return out

    def landed(copies):
        for copy in copies:
            copy.wait_recv()

    def sum_along(s, a, value):
        cur[s, a] = value
        slots[s, a, me[a]] = value
        out = []
        for k in (1, 2, 3):
            n = 7 + a * 3 + k
            out.append(remote(cur.at[s, a], slots.at[s, a, me[a]], sum_send.at[s, n], sum_recv.at[s, n],
                              device(moved(a, k), core)))
        return out

    def sum_first(s, copies):
        landed(copies)
        v = [first[s, n] for n in range(8)]
        return ((v[0] + v[1]) + (v[2] + v[3])) + ((v[4] + v[5]) + (v[6] + v[7]))

    def sum_next(s, a, copies):
        landed(copies)
        return (slots[s, a, 0] + slots[s, a, 1]) + (slots[s, a, 2] + slots[s, a, 3])

    def sum_spread(s, value):
        cur[s, 2] = value
        total[s, mine, :] = value
        out = []
        for dx, dc in near:
            n = 13 + dx * 2 + dc
            out.append(remote(cur.at[s, 2], total.at[s, mine], sum_send.at[s, n], sum_recv.at[s, n],
                              near_device(dx, dc)))
        return out

    ring = {}

    def half(h):
        return pl.ds(2 * h, 2)

    def view(phase, p, q, coord, h):
        a, b, c = ORDERS[p]
        if phase == 0:
            return acc.at[place(p, coord, around(b, q), half(h))]
        return acc.at[place(p, me[a], coord, half(h))]

    def box(phase, p, q, m, h):
        nr = PARTS[p][1]
        if phase == 0:
            return box1.at[p, q, m, :, pl.ds(0, nr)]
        return box2.at[p, m, :, pl.ds(0, nr)]

    def send(phase, p, q, m):
        axis = ORDERS[p][phase]
        sign = 1 if m % 2 == 0 else -1
        h = TURN[m]
        n = (p * 4 + q) * 6 + m if phase == 0 else 72 + (phase - 1) * 18 + p * 6 + m
        ring[phase, p, q, m] = remote(
            view(phase, p, q, around(axis, 2 if m < 2 else sign), h), box(phase, p, q, m, h),
            ring_send.at[n], ring_recv.at[n], device(moved(axis, sign), core))

    def relay(phase, p, q, m):
        axis = ORDERS[p][phase]
        sign = 1 if m == 0 else -1
        ring[phase, p, q, m].wait_recv()
        add(view(phase, p, q, around(axis, sign), m), box(phase, p, q, m, m), 2)
        send(phase, p, q, 4 + m)

    def land(phase, p, q, m):
        ring[phase, p, q, m].wait_recv()
        add(view(phase, p, q, me[ORDERS[p][phase]], TURN[m]), box(phase, p, q, m, TURN[m]), 2)

    def open_far(q):
        for p in range(3):
            merge(2, q, p)
            send(0, p, q, 0)
            send(0, p, q, 1)

    def open_near(q):
        for p in range(3):
            merge(1, q, p)
            send(0, p, q, 2)
            merge(3, q, p)
            send(0, p, q, 3)

    def open_round(q):
        open_far(q)
        open_near(q)

    def relay_round(q):
        for p in range(3):
            relay(0, p, q, 0)
            relay(0, p, q, 1)

    def close_round(q):
        for p in range(3):
            merge(0, q, p)
        for m in (2, 3, 4, 5):
            for p in range(3):
                land(0, p, q, m)
        for p in range(3):
            if q == 2:
                send(1, p, 0, 0)
                send(1, p, 0, 1)
            elif q == 1:
                send(1, p, 0, 2)
            elif q == 3:
                send(1, p, 0, 3)
        if q in (1, 3):
            for p in range(3):
                relay(1, p, 0, 0 if q == 1 else 1)

    for k in ROUNDS:
        for p in range(3):
            piece(k, 2, p)

    open_far(2)

    def gram_body(i, g):
        v = split[pl.ds(i * 8, 8)].reshape(8 * TILE, 2 * SKETCH)
        return split_gram(v, g)
    g = lax.fori_loop(0, CB_DEV // 8, gram_body, jnp.zeros((2 * SKETCH, 2 * SKETCH), F32))
    gram[0] = fold(g)
    copies = sum_start(0)
    for q in ROUNDS[1:]:
        for k in ROUNDS:
            for p in range(3):
                piece(k, q, p)

    open_near(2)
    open_round(1)
    copies = sum_along(0, 1, sum_first(0, copies))
    relay_round(2)
    open_round(3)
    copies = sum_along(0, 0, sum_next(0, 1, copies))
    relay_round(1)
    close_round(2)
    copies = sum_spread(0, sum_next(0, 0, copies))
    open_round(0)
    relay_round(3)
    close_round(1)
    landed(copies)
    factor_start(total.at[0], work)
    factor_steps(work, inv1, 0, 5)
    relay_round(0)
    factor_steps(work, inv1, 5, 10)
    close_round(3)
    factor_steps(work, inv1, 10, 16)
    close_round(0)
    for m in (2, 3, 4, 5):
        for p in range(3):
            land(1, p, 0, m)
    last = {}
    for k in (2, 1, 3):
        for p in range(3):
            a, b, c = ORDERS[p]
            n = 90 + p * 3 + k - 1
            last[p, k] = remote(acc.at[place(p, me[a], me[b], around(c, k))],
                                box3.at[p, k - 1, pl.ds(0, PARTS[p][1])],
                                ring_send.at[n], ring_recv.at[n], device(moved(c, k), core))
    weights = split_weights(inv1[...] * scale)
    for p in range(3):
        a, b, c = ORDERS[p]
        nr = PARTS[p][1]
        for k in (1, 3, 2):
            last[p, k].wait_recv()
        own = acc.at[place(p, me[a], me[b], me[c])]
        own[...] = (own[...] + box3[p, 0, :nr]) + (box3[p, 1, :nr] + box3[p, 2, :nr])

    zv = split_dot(jnp.concatenate(cut_two(acc[z, y, x]), axis=1), weights) * (1.0 / scale)
    zv = jnp.concatenate(cut_two(zv), axis=1)
    zed[...] = zv
    gram[1] = fold(split_gram(zv, jnp.zeros((2 * SKETCH, 2 * SKETCH), F32)))

    def cells(n):
        def body(i, carry):
            v = split[pl.ds(i * 4, 4)].reshape(4 * TILE, 2 * SKETCH)
            cell[pl.ds(pl.multiple_of(i * 4 * TILE, 4 * TILE), 4 * TILE), :] = split_dot(v, weights).astype(BF16)
            return carry
        lax.fori_loop(n * 4, n * 4 + 4, body, 0)

    copies = sum_start(1)
    cells(0)
    copies = sum_along(1, 1, sum_first(1, copies))
    cells(1)
    copies = sum_along(1, 0, sum_next(1, 1, copies))
    cells(2)
    copies = sum_spread(1, sum_next(1, 0, copies))
    cells(3)
    landed(copies)
    total2[...] = total[1]
    for copy in sends:
        copy.wait_send()


def finish_kernel(cell, zed, gram, cell_out, gene_out, work, inv2, out_sem):
    copy = pltpu.make_async_copy(cell, cell_out, out_sem.at[0])
    copy.start()
    factor_start(gram, work)
    for n in range(4):
        factor_steps(work, inv2, n * 4, n * 4 + 4)
    gene_out[...] = split_dot(zed[...], split_weights(inv2[...] * math.sqrt(GENES)))
    copy.wait()


def exchange(split, w):
    vmem = pl.BlockSpec(memory_space=pltpu.VMEM)
    sq = (SKETCH, SKETCH)
    part = (SKETCH // 8, SKETCH)
    return pl.pallas_call(
        exchange_kernel,
        name="exchange",
        out_shape=(
            pltpu.VMEM((CB_DEV * TILE, SKETCH), BF16),
            pltpu.VMEM((2 * TILE, 2 * SKETCH), BF16),
            pltpu.VMEM(sq, F32),
        ),
        in_specs=[vmem, vmem],
        out_specs=(vmem, vmem, vmem),
        scratch_shapes=[
            pltpu.VMEM((4, 4, 4, 2 * TILE, SKETCH), F32),
            pltpu.VMEM((3, 4, 6, 2, 88, SKETCH), F32),
            pltpu.VMEM((3, 6, 2, 88, SKETCH), F32),
            pltpu.VMEM((3, 3, 88, SKETCH), F32),
            pltpu.VMEM((2,) + sq, F32),
            pltpu.VMEM((2,) + sq, F32),
            pltpu.VMEM((SKETCH, 2 * SKETCH), F32),
            pltpu.VMEM(sq, F32),
            pltpu.VMEM((2, 3) + part, F32),
            pltpu.VMEM((2, 8) + part, F32),
            pltpu.VMEM((2, 2, 4) + part, F32),
            pltpu.SemaphoreType.DMA((48,)),
            pltpu.SemaphoreType.DMA((48,)),
            pltpu.SemaphoreType.DMA((99,)),
            pltpu.SemaphoreType.DMA((99,)),
            pltpu.SemaphoreType.DMA((2, 21)),
            pltpu.SemaphoreType.DMA((2, 21)),
        ],
        compiler_params=pltpu.CompilerParams(
            collective_id=0, has_side_effects=True, vmem_limit_bytes=26 << 20),
    )(pltpu.with_memory_space_constraint(split, pltpu.VMEM), pltpu.with_memory_space_constraint(w, pltpu.VMEM))


def finish(cell, zed, gram):
    vmem = pl.BlockSpec(memory_space=pltpu.VMEM)
    held = [pltpu.with_memory_space_constraint(v, pltpu.VMEM) for v in (cell, zed, gram)]
    return pl.pallas_call(
        finish_kernel,
        name="finish",
        out_shape=(
            jax.ShapeDtypeStruct((CB_DEV * TILE, SKETCH), BF16),
            jax.ShapeDtypeStruct((2 * TILE, SKETCH), F32),
        ),
        in_specs=[vmem, vmem, vmem],
        out_specs=(pl.BlockSpec(memory_space=pl.ANY), vmem),
        scratch_shapes=[
            pltpu.VMEM((SKETCH, 2 * SKETCH), F32),
            pltpu.VMEM((SKETCH, SKETCH), F32),
            pltpu.SemaphoreType.DMA((1,)),
        ],
        compiler_params=pltpu.CompilerParams(vmem_limit_bytes=26 << 20),
    )(*held)


def on_device(tiles, tile_rows, tile_cols, tile_counts, block_order, sketch):
    split, w = local_pass(tiles, tile_rows, tile_cols, tile_counts, block_order, sketch)
    return finish(*exchange(split, w))


def solution(mesh):
    placed = (
        P(("gx", "gy"), None, None),
        P(("gx", "gy")),
        P(("gx", "gy")),
        P(("gx", "gy")),
        P(),
        P(),
    )
    return jax.shard_map(
        on_device,
        mesh=mesh,
        in_specs=placed,
        out_specs=(P(("gx", "gy"), None), P(("gx", "gy"), None)),
        check_vma=False,
    )
```

```python
import math

import jax
import jax.numpy as jnp
from jax import lax
from jax.experimental import pallas as pl
from jax.experimental.pallas import tpu as pltpu
from jax.sharding import PartitionSpec as P

TILE = 128
SKETCH = 128
GENES = 32768
CB_DEV = 64
BLOCKS = 256
SLOTS = 192
GROUP = 64
CHUNK = 64
F32 = jnp.float32
BF16 = jnp.bfloat16


def local_kernel(counts, rows_hbm, cols_hbm, order_hbm, tiles_hbm, sketch_hbm, split, w_out,
                 tiles, sketch, y_ref, place, rows, cols, order,
                 tile_sems, sketch_sems, index_sems):
    lists = ((rows_hbm, rows), (cols_hbm, cols), (order_hbm, order))
    index_copies = [pltpu.make_async_copy(a, b, index_sems.at[i]) for i, (a, b) in enumerate(lists)]
    for copy in index_copies:
        copy.start()
    w_ref = w_out.reshape(BLOCKS, TILE, SKETCH)
    n_tile = SLOTS // CHUNK
    n_sk = 4
    sk = GENES // n_sk

    def tile_copy(i):
        return pltpu.make_async_copy(
            tiles_hbm.at[pl.ds(i * CHUNK, CHUNK)], tiles.at[pl.ds(i * CHUNK, CHUNK)], tile_sems.at[i])

    def sketch_copy(i):
        return pltpu.make_async_copy(
            sketch_hbm.at[pl.ds(i * sk, sk)], sketch.at[pl.ds(i * sk, sk)], sketch_sems.at[i])

    for i in range(n_sk):
        sketch_copy(i).start()
    for i in range(n_tile):
        tile_copy(i).start()

    for copy in index_copies:
        copy.wait()
    live = counts[0]

    def invert(i, _):
        for u in range(8):
            place[order[i * 8 + u]] = i * 8 + u
        return 0
    lax.fori_loop(0, BLOCKS // 8, invert, 0)

    def clear_y(i, _):
        for u in range(4):
            y_ref[i * 4 + u] = jnp.zeros((TILE, SKETCH), F32)
        return 0
    lax.fori_loop(0, CB_DEV // 4, clear_y, 0)

    def clear_w(i, _):
        for u in range(4):
            w_ref[i * 4 + u] = jnp.zeros((TILE, SKETCH), F32)
        return 0
    lax.fori_loop(0, BLOCKS // 4, clear_w, 0)

    for i in range(n_sk):
        sketch_copy(i).wait()

    def cells(i):
        base = i * GROUP
        parts = []
        for u in range(GROUP):
            c = pl.multiple_of(cols[base + u] * TILE, TILE)
            p = jnp.dot(tiles[base + u], sketch[pl.ds(c, TILE), :], preferred_element_type=F32)
            parts.append(jnp.where(base + u < live, p, 0.0))
        for u in range(GROUP):
            r = rows[base + u]
            y_ref[r] = y_ref[r] + parts[u]

    def cell_body(i, _):
        @pl.when(i % (CHUNK // GROUP) == 0)
        def _():
            tile_copy(i // (CHUNK // GROUP)).wait()
        cells(i)
        return 0
    steps = (live + GROUP - 1) // GROUP
    lax.fori_loop(0, steps, cell_body, 0)

    def late(i, _):
        tile_copy(i).wait()
        return 0
    lax.fori_loop((live + CHUNK - 1) // CHUNK, n_tile, late, 0)

    def cut(i, _):
        for u in range(4):
            v = y_ref[i * 4 + u]
            hi = v.astype(BF16)
            split[i * 4 + u, :, :SKETCH] = hi
            split[i * 4 + u, :, SKETCH:] = (v - hi.astype(F32)).astype(BF16)
        return 0
    lax.fori_loop(0, CB_DEV // 4, cut, 0)

    def gene_body(i, _):
        base = i * GROUP
        parts = []
        for u in range(GROUP):
            r = rows[base + u]
            p = lax.dot_general(tiles[base + u], split[r], (((0,), (0,)), ((), ())),
                                preferred_element_type=F32)
            v = p[:, :SKETCH] + p[:, SKETCH:]
            parts.append(jnp.where(base + u < live, v, 0.0))
        for u in range(GROUP):
            o = place[cols[base + u]]
            w_ref[o] = w_ref[o] + parts[u]
        return 0
    lax.fori_loop(0, steps, gene_body, 0)


def local_pass(tiles, rows, cols, counts, order, sketch):
    hbm = [pltpu.with_memory_space_constraint(v, pltpu.HBM) for v in (rows, cols, order, tiles, sketch)]
    anyp = pl.BlockSpec(memory_space=pl.ANY)
    vmem = pl.BlockSpec(memory_space=pltpu.VMEM)
    return pl.pallas_call(
        local_kernel,
        name="local_pass",
        out_shape=(
            pltpu.VMEM((CB_DEV, TILE, 2 * SKETCH), BF16),
            pltpu.VMEM((4, 2, 4, 4, 2 * TILE, SKETCH), F32),
        ),
        in_specs=[pl.BlockSpec(memory_space=pltpu.SMEM)] + [anyp] * 5,
        out_specs=(vmem, vmem),
        scratch_shapes=[
            pltpu.VMEM((SLOTS, TILE, TILE), BF16),
            pltpu.VMEM((GENES, SKETCH), BF16),
            pltpu.VMEM((CB_DEV, TILE, SKETCH), F32),
            pltpu.SMEM((BLOCKS,), jnp.int32),
            pltpu.SMEM((SLOTS,), jnp.int32),
            pltpu.SMEM((SLOTS,), jnp.int32),
            pltpu.SMEM((BLOCKS,), jnp.int32),
            pltpu.SemaphoreType.DMA((SLOTS // CHUNK,)),
            pltpu.SemaphoreType.DMA((4,)),
            pltpu.SemaphoreType.DMA((4,)),
        ],
        compiler_params=pltpu.CompilerParams(vmem_limit_bytes=26 << 20),
    )(counts, *hbm)


PARTS = ((0, 88), (88, 88), (176, 80))
ORDERS = ((2, 1, 0), (1, 0, 2), (0, 2, 1))
ROUNDS = (2, 1, 3, 0)
TURN = (0, 1, 1, 0, 0, 1)
MESH = pl.DeviceIdType.MESH


def cut_two(v):
    hi = v.astype(BF16)
    return hi, (v - hi.astype(F32)).astype(BF16)


WINDOW = 4


def split_weights(inverse):
    hi, lo = cut_two(inverse)
    return jnp.concatenate(
        [jnp.concatenate([hi, hi], axis=1), jnp.concatenate([lo, jnp.zeros_like(lo)], axis=1)], axis=0)


def split_dot(terms, weights):
    o = lax.dot_general(terms, weights, (((1,), (1,)), ((), ())), preferred_element_type=F32)
    return o[:, :SKETCH] + o[:, SKETCH:]


def split_gram(terms, g):
    g = g + lax.dot_general(terms, terms, (((0,), (0,)), ((), ())), preferred_element_type=F32)
    return g


def fold(g):
    return (g[:SKETCH, :SKETCH] + g[SKETCH:, SKETCH:]) + (g[:SKETCH, SKETCH:] + g[SKETCH:, :SKETCH])


def factor_start(gram, work):
    work[:, :SKETCH] = gram[...]
    ri = lax.broadcasted_iota(jnp.int32, (SKETCH, SKETCH), 0)
    ci = lax.broadcasted_iota(jnp.int32, (SKETCH, SKETCH), 1)
    work[:, SKETCH:] = jnp.where(ri == ci, 1.0, 0.0)


def factor_steps(work, out, first, last):
    rows = 32
    down = lax.broadcasted_iota(jnp.int32, (rows, 1), 0)

    def lane(v, n):
        return jnp.broadcast_to(v[:, n:n + 1], (v.shape[0], SKETCH))

    def group(j, l0):
        tile = pl.ds(pl.multiple_of(j, 8), 8)
        lt = work[tile, :SKETCH]
        rt = work[tile, SKETCH:]
        left = [jnp.broadcast_to(lt[l0 + t:l0 + t + 1], (8, SKETCH)) for t in range(WINDOW)]
        right = [jnp.broadcast_to(rt[l0 + t:l0 + t + 1], (8, SKETCH)) for t in range(WINDOW)]
        e = {(s, t): lane(left[s], l0 + t) for s in range(WINDOW) for t in range(s, WINDOW)}
        w = {}
        inv = []
        for s in range(WINDOW):
            inv.append(1.0 / e[s, s])
            for t in range(s + 1, WINDOW):
                w[s, t] = e[s, t] * inv[s]
            for t in range(s + 1, WINDOW):
                for u in range(t, WINDOW):
                    e[t, u] = e[t, u] - w[s, t] * e[s, u]
                left[t] = left[t] - w[s, t] * left[s]
                right[t] = right[t] - w[s, t] * right[s]
        done = [right[t] * (1.0 / jnp.sqrt(e[t, t])) for t in range(WINDOW)]
        ql = [(left[t] * inv[t])[:1] for t in range(WINDOW)]
        qr = [(right[t] * inv[t])[:1] for t in range(WINDOW)]
        ww = {k: v[:1] for k, v in w.items()}
        for i in range(first * 8 // rows, SKETCH // rows):
            here = pl.ds(i * rows, rows)
            a = work[here, :SKETCH]
            b = work[here, SKETCH:]
            below = down + i * rows > j + l0 + WINDOW - 1
            c = [jnp.where(below, lane(a, l0 + t), 0.0) for t in range(WINDOW)]
            for t in range(1, WINDOW):
                for s in range(t):
                    c[t] = c[t] - c[s] * ww[s, t]
            for t in range(WINDOW):
                a = a - c[t] * ql[t]
                b = b - c[t] * qr[t]
            if l0 + WINDOW == 8:
                a = pltpu.roll(a, SKETCH - 8, 1)
            work[here, :SKETCH] = a
            work[here, SKETCH:] = b
        return done

    sub = lax.broadcasted_iota(jnp.int32, (8, 1), 0)

    def body(i, carry):
        done = []
        for l0 in range(0, 8, WINDOW):
            done += group(i * 8, l0)
        tile = done[0]
        for t in range(1, 8):
            tile = jnp.where(sub == t, done[t], tile)
        out[pl.ds(pl.multiple_of(i * 8, 8), 8), :] = tile
        return carry

    lax.fori_loop(first, last, body, 0)


def exchange_kernel(split, w, cell, zed, total2,
                    acc, box1, box2, box3, gram, total, work, inv1,
                    cur, first, slots,
                    in_send, in_recv, ring_send, ring_recv, sum_send, sum_recv):
    gx = lax.axis_index("gx")
    gy = lax.axis_index("gy")
    z, core = gx // 2, gx % 2
    y, x = gy // 4, gy % 4
    me = (z, y, x)

    def device(pos, c):
        return (pos[0] * 2 + c, pos[1] * 4 + pos[2])

    def around(axis, k):
        return (me[axis] + k + 4) % 4

    def moved(axis, k):
        pos = list(me)
        pos[axis] = around(axis, k)
        return pos

    near = [(dx, dc) for dx in range(4) for dc in range(2) if dx or dc]

    def near_device(dx, dc):
        return device(moved(2, dx), 1 - core if dc else core)

    partner = near_device(0, 1)
    barrier = pltpu.get_barrier_semaphore()
    peers = [near_device(dx, dc) for dx, dc in near]
    peers += [device(moved(a, k), core) for a in (0, 1) for k in (1, 2, 3)]
    for peer in peers:
        pl.semaphore_signal(barrier, inc=1, device_id=peer, device_id_type=MESH)
    pl.semaphore_wait(barrier, len(peers))

    scale = math.sqrt(CB_DEV * TILE * 128)
    sends = []

    def remote(src, dst, send, recv, peer):
        copy = pltpu.make_async_remote_copy(
            src_ref=src, dst_ref=dst, send_sem=send, recv_sem=recv,
            device_id=peer, device_id_type=MESH)
        copy.start()
        sends.append(copy)
        return copy

    def add(dst, src, lead):
        def body(i, carry):
            dst[i] = dst[i] + src[i]
            return carry
        lax.fori_loop(0, lead, body, 0)

    def place(p, ca, cb, cc):
        idx = [None] * 3
        for d, v in zip(ORDERS[p], (ca, cb, cc)):
            idx[d] = v
        r0, nr = PARTS[p]
        return tuple(idx) + (pl.ds(r0, nr),)

    def with_core(idx, c):
        return (idx[0], c) + tuple(idx[1:])

    pieces = {}

    def piece(k, q, p):
        n = (k * 4 + q) * 3 + p
        a, b = ORDERS[p][:2]
        idx = place(p, around(a, k), around(b, q), slice(None))
        pieces[k, q, p] = idx, remote(w.at[with_core(idx, 1 - core)], acc.at[idx],
                                      in_send.at[n], in_recv.at[n], partner)

    def merge(k, q, p):
        idx, copy = pieces[k, q, p]
        copy.wait_recv()
        add(acc.at[idx], w.at[with_core(idx, core)], 4)

    share = SKETCH // 8
    mine = pl.ds((x * 2 + core) * share, share)

    def sum_start(s):
        first[s, x * 2 + core] = gram[s, mine, :]
        out = []
        for dx, dc in near:
            n = dx * 2 + dc
            to = around(2, dx) * 2 + ((1 - core) if dc else core)
            out.append(remote(gram.at[s, pl.ds(to * share, share)], first.at[s, x * 2 + core],
                              sum_send.at[s, n], sum_recv.at[s, n], near_device(dx, dc)))
        return out

    def landed(copies):
        for copy in copies:
            copy.wait_recv()

    def sum_along(s, a, value):
        cur[s, a] = value
        slots[s, a, me[a]] = value
        out = []
        for k in (1, 2, 3):
            n = 7 + a * 3 + k
            out.append(remote(cur.at[s, a], slots.at[s, a, me[a]], sum_send.at[s, n], sum_recv.at[s, n],
                              device(moved(a, k), core)))
        return out

    def sum_first(s, copies):
        landed(copies)
        v = [first[s, n] for n in range(8)]
        return ((v[0] + v[1]) + (v[2] + v[3])) + ((v[4] + v[5]) + (v[6] + v[7]))

    def sum_next(s, a, copies):
        landed(copies)
        return (slots[s, a, 0] + slots[s, a, 1]) + (slots[s, a, 2] + slots[s, a, 3])

    def sum_spread(s, value):
        cur[s, 2] = value
        total[s, mine, :] = value
        out = []
        for dx, dc in near:
            n = 13 + dx * 2 + dc
            out.append(remote(cur.at[s, 2], total.at[s, mine], sum_send.at[s, n], sum_recv.at[s, n],
                              near_device(dx, dc)))
        return out

    ring = {}

    def half(h):
        return pl.ds(2 * h, 2)

    def view(phase, p, q, coord, h):
        a, b, c = ORDERS[p]
        if phase == 0:
            return acc.at[place(p, coord, around(b, q), half(h))]
        return acc.at[place(p, me[a], coord, half(h))]

    def box(phase, p, q, m, h):
        nr = PARTS[p][1]
        if phase == 0:
            return box1.at[p, q, m, :, pl.ds(0, nr)]
        return box2.at[p, m, :, pl.ds(0, nr)]

    def send(phase, p, q, m):
        axis = ORDERS[p][phase]
        sign = 1 if m % 2 == 0 else -1
        h = TURN[m]
        n = (p * 4 + q) * 6 + m if phase == 0 else 72 + (phase - 1) * 18 + p * 6 + m
        ring[phase, p, q, m] = remote(
            view(phase, p, q, around(axis, 2 if m < 2 else sign), h), box(phase, p, q, m, h),
            ring_send.at[n], ring_recv.at[n], device(moved(axis, sign), core))

    def relay(phase, p, q, m):
        axis = ORDERS[p][phase]
        sign = 1 if m == 0 else -1
        ring[phase, p, q, m].wait_recv()
        add(view(phase, p, q, around(axis, sign), m), box(phase, p, q, m, m), 2)
        send(phase, p, q, 4 + m)

    def land(phase, p, q, m):
        ring[phase, p, q, m].wait_recv()
        add(view(phase, p, q, me[ORDERS[p][phase]], TURN[m]), box(phase, p, q, m, TURN[m]), 2)

    def open_far(q):
        for p in range(3):
            merge(2, q, p)
            send(0, p, q, 0)
            send(0, p, q, 1)

    def open_near(q):
        for p in range(3):
            merge(1, q, p)
            send(0, p, q, 2)
            merge(3, q, p)
            send(0, p, q, 3)

    def open_round(q):
        open_far(q)
        open_near(q)

    def relay_round(q):
        for p in range(3):
            relay(0, p, q, 0)
            relay(0, p, q, 1)

    def close_round(q):
        for p in range(3):
            merge(0, q, p)
        for m in (2, 3, 4, 5):
            for p in range(3):
                land(0, p, q, m)
        for p in range(3):
            if q == 2:
                send(1, p, 0, 0)
                send(1, p, 0, 1)
            elif q == 1:
                send(1, p, 0, 2)
            elif q == 3:
                send(1, p, 0, 3)
        if q in (1, 3):
            for p in range(3):
                relay(1, p, 0, 0 if q == 1 else 1)

    for k in ROUNDS:
        for p in range(3):
            piece(k, 2, p)

    open_far(2)

    def gram_body(i, g):
        v = split[pl.ds(i * 32, 32)].reshape(32 * TILE, 2 * SKETCH)
        return split_gram(v, g)
    g = lax.fori_loop(0, CB_DEV // 32, gram_body, jnp.zeros((2 * SKETCH, 2 * SKETCH), F32))
    gram[0] = fold(g)
    copies = sum_start(0)
    for q in ROUNDS[1:]:
        for k in ROUNDS:
            for p in range(3):
                piece(k, q, p)

    open_near(2)
    open_round(1)
    copies = sum_along(0, 1, sum_first(0, copies))
    relay_round(2)
    open_round(3)
    copies = sum_along(0, 0, sum_next(0, 1, copies))
    relay_round(1)
    close_round(2)
    copies = sum_spread(0, sum_next(0, 0, copies))
    open_round(0)
    relay_round(3)
    close_round(1)
    landed(copies)
    factor_start(total.at[0], work)
    factor_steps(work, inv1, 0, 5)
    relay_round(0)
    factor_steps(work, inv1, 5, 10)
    close_round(3)
    factor_steps(work, inv1, 10, 16)
    close_round(0)
    for m in (2, 3, 4, 5):
        for p in range(3):
            land(1, p, 0, m)
    last = {}
    for k in (2, 1, 3):
        for p in range(3):
            a, b, c = ORDERS[p]
            n = 90 + p * 3 + k - 1
            last[p, k] = remote(acc.at[place(p, me[a], me[b], around(c, k))],
                                box3.at[p, k - 1, pl.ds(0, PARTS[p][1])],
                                ring_send.at[n], ring_recv.at[n], device(moved(c, k), core))
    weights = split_weights(inv1[...] * scale)
    for p in range(3):
        a, b, c = ORDERS[p]
        nr = PARTS[p][1]
        for k in (1, 3, 2):
            last[p, k].wait_recv()
        own = acc.at[place(p, me[a], me[b], me[c])]
        own[...] = (own[...] + box3[p, 0, :nr]) + (box3[p, 1, :nr] + box3[p, 2, :nr])

    zv = split_dot(jnp.concatenate(cut_two(acc[z, y, x]), axis=1), weights) * (1.0 / scale)
    zv = jnp.concatenate(cut_two(zv), axis=1)
    zed[...] = zv
    gram[1] = fold(split_gram(zv, jnp.zeros((2 * SKETCH, 2 * SKETCH), F32)))

    def cells(n):
        def body(i, carry):
            v = split[pl.ds(i * 4, 4)].reshape(4 * TILE, 2 * SKETCH)
            cell[pl.ds(pl.multiple_of(i * 4 * TILE, 4 * TILE), 4 * TILE), :] = split_dot(v, weights).astype(BF16)
            return carry
        lax.fori_loop(n * 4, n * 4 + 4, body, 0)

    copies = sum_start(1)
    cells(0)
    copies = sum_along(1, 1, sum_first(1, copies))
    cells(1)
    copies = sum_along(1, 0, sum_next(1, 1, copies))
    cells(2)
    copies = sum_spread(1, sum_next(1, 0, copies))
    cells(3)
    landed(copies)
    total2[...] = total[1]
    for copy in sends:
        copy.wait_send()


def finish_kernel(cell, zed, gram, cell_out, gene_out, work, inv2, out_sem):
    copy = pltpu.make_async_copy(cell, cell_out, out_sem.at[0])
    copy.start()
    factor_start(gram, work)
    for n in range(4):
        factor_steps(work, inv2, n * 4, n * 4 + 4)
    gene_out[...] = split_dot(zed[...], split_weights(inv2[...] * math.sqrt(GENES)))
    copy.wait()


def exchange(split, w):
    vmem = pl.BlockSpec(memory_space=pltpu.VMEM)
    sq = (SKETCH, SKETCH)
    part = (SKETCH // 8, SKETCH)
    return pl.pallas_call(
        exchange_kernel,
        name="exchange",
        out_shape=(
            pltpu.VMEM((CB_DEV * TILE, SKETCH), BF16),
            pltpu.VMEM((2 * TILE, 2 * SKETCH), BF16),
            pltpu.VMEM(sq, F32),
        ),
        in_specs=[vmem, vmem],
        out_specs=(vmem, vmem, vmem),
        scratch_shapes=[
            pltpu.VMEM((4, 4, 4, 2 * TILE, SKETCH), F32),
            pltpu.VMEM((3, 4, 6, 2, 88, SKETCH), F32),
            pltpu.VMEM((3, 6, 2, 88, SKETCH), F32),
            pltpu.VMEM((3, 3, 88, SKETCH), F32),
            pltpu.VMEM((2,) + sq, F32),
            pltpu.VMEM((2,) + sq, F32),
            pltpu.VMEM((SKETCH, 2 * SKETCH), F32),
            pltpu.VMEM(sq, F32),
            pltpu.VMEM((2, 3) + part, F32),
            pltpu.VMEM((2, 8) + part, F32),
            pltpu.VMEM((2, 2, 4) + part, F32),
            pltpu.SemaphoreType.DMA((48,)),
            pltpu.SemaphoreType.DMA((48,)),
            pltpu.SemaphoreType.DMA((99,)),
            pltpu.SemaphoreType.DMA((99,)),
            pltpu.SemaphoreType.DMA((2, 21)),
            pltpu.SemaphoreType.DMA((2, 21)),
        ],
        compiler_params=pltpu.CompilerParams(
            collective_id=0, has_side_effects=True, vmem_limit_bytes=26 << 20),
    )(pltpu.with_memory_space_constraint(split, pltpu.VMEM), pltpu.with_memory_space_constraint(w, pltpu.VMEM))


def finish(cell, zed, gram):
    vmem = pl.BlockSpec(memory_space=pltpu.VMEM)
    held = [pltpu.with_memory_space_constraint(v, pltpu.VMEM) for v in (cell, zed, gram)]
    return pl.pallas_call(
        finish_kernel,
        name="finish",
        out_shape=(
            jax.ShapeDtypeStruct((CB_DEV * TILE, SKETCH), BF16),
            jax.ShapeDtypeStruct((2 * TILE, SKETCH), F32),
        ),
        in_specs=[vmem, vmem, vmem],
        out_specs=(pl.BlockSpec(memory_space=pl.ANY), vmem),
        scratch_shapes=[
            pltpu.VMEM((SKETCH, 2 * SKETCH), F32),
            pltpu.VMEM((SKETCH, SKETCH), F32),
            pltpu.SemaphoreType.DMA((1,)),
        ],
        compiler_params=pltpu.CompilerParams(vmem_limit_bytes=26 << 20),
    )(*held)


def on_device(tiles, tile_rows, tile_cols, tile_counts, block_order, sketch):
    split, w = local_pass(tiles, tile_rows, tile_cols, tile_counts, block_order, sketch)
    return finish(*exchange(split, w))


def solution(mesh):
    placed = (
        P(("gx", "gy"), None, None),
        P(("gx", "gy")),
        P(("gx", "gy")),
        P(("gx", "gy")),
        P(),
        P(),
    )
    return jax.shard_map(
        on_device,
        mesh=mesh,
        in_specs=placed,
        out_specs=(P(("gx", "gy"), None), P(("gx", "gy"), None)),
        check_vma=False,
    )
```
